512 devices in a mesh: dp: 8 (over z), dom: 64 (over y, x, core).
Axes of the slice: x: 4, y: 8, z: 8, core: 2. Of those that a mesh axis runs over, the one named last changes fastest.
Arguments:
- features: bfloat16 [8, 65536, 256], P('dp', 'dom'), may hold values from -6 to 6
- send_order: int32 [64, 1024], P('dom'), may hold values from 0 to 1023, each once within a row
- adj_count: int32 [512], P('dom'), may hold values from 2 to 4, as said below
- adj_target: int32 [512, 4], P('dom'), may hold values from 6 to 17, as said below
- adj_vals: bfloat16 [512, 4, 128, 128], P('dom'), may hold values from -0.3125 to 0.3125
- w_edge: bfloat16 [256, 256], replicated, may hold values from -0.375 to 0.375
- w_node: bfloat16 [512, 256], replicated, may hold values from -0.25 to 0.25
- cotangent: bfloat16 [8, 65536, 256], P('dp', 'dom'), may hold values from -6 to 6
Outputs:
- node_out: bfloat16 [8, 65536, 256], P('dp', 'dom')
- grad_features: bfloat16 [8, 65536, 256], P('dp', 'dom')
- grad_edge: float32 [256, 256], replicated
- grad_node: float32 [512, 256], replicated
The draws below stay inside these ranges and needn't reach their ends.
Inputs may be any that keep to these rules, and one draw needn't show every extreme that they name: Each row of send_order is a permutation of 0 to 1023. `adj_count`: every partition has its own most count, reached by one of its blocks; some partition's most is 4. `adj_target`: targets lie in the own partition's blocks or in the last 2 blocks of the previous partition or the first 2 blocks of the next one; slot 0 of each partition's first column block targets the previous partition, and slot 1 of its last column block targets the next one.
All inputs are finite; a program needn't handle non-finite values.
Results may differ from the reference program's by a relative error of at most 0.009.
Values may be sent and summed in bfloat16 or wider, within the bound.
A program may use at most 64 MiB of HBM per device.

```python
import jax
import jax.numpy as jnp
from jax import lax

H = 256
NODES_DEV = 1024
NB = 4
RIM = 2
NODES = 65536
BLK = 8
NBLOCKS = 512
PER_PEER = 16
N_DP = 8
N_DOM = 64


def draw_adj_count(key, part):
    key_cap = jax.random.fold_in(key, 11)
    key_top = jax.random.fold_in(key, 12)
    key_cnt = jax.random.fold_in(key, 13)
    caps = jax.random.randint(key_cap, (N_DOM,), 2, NB + 1)
    top = jax.random.randint(key_top, (), 0, N_DOM)
    caps = jnp.where(jnp.arange(N_DOM) == top, NB, caps)
    counts = jax.random.randint(key_cnt, (N_DOM, BLK), 2, caps[:, None] + 1)
    counts = jnp.where(jnp.arange(BLK)[None, :] == 0, caps[:, None], counts)
    return counts.reshape(-1).astype(jnp.int32)


def draw_adj_target(key, part):
    key_reg = jax.random.fold_in(key, 21)
    key_off = jax.random.fold_in(key, 22)
    key_own = jax.random.fold_in(key, 23)
    region = jax.random.randint(key_reg, (NBLOCKS, NB), 0, 6)
    offset = jax.random.randint(key_off, (NBLOCKS, NB), 0, RIM)
    own = jax.random.randint(key_own, (NBLOCKS, NB), BLK, 2 * BLK)
    local = (jnp.arange(NBLOCKS) % BLK)[:, None]
    slot = jnp.arange(NB)[None, :]
    region = jnp.where((local == 0) & (slot == 0), 0, region)
    region = jnp.where((local == BLK - 1) & (slot == 1), 1, region)
    target = jnp.where(region == 0, BLK - RIM + offset, jnp.where(region == 1, 2 * BLK + offset, own))
    return target.astype(jnp.int32)


def block_levels(key, shape, cuts, least, high):
    gain = 1.0
    for position, parts in cuts:
        heights = jax.random.uniform(jax.random.fold_in(jax.random.fold_in(key, 6), position), (parts,), jnp.float32, least / len(cuts), high / len(cuts))
        gain = gain * jnp.repeat(jnp.exp(heights), shape[position] // parts).reshape((-1,) + (1,) * (len(shape) - 1 - position))
    return gain


def bell_draw(stream_key, shape, width, bound, shards=(), kind=jnp.bfloat16):
    gain = block_levels(stream_key, shape, shards, -0.22, 0.18) if shards else 1.0
    entries = jax.random.normal(stream_key, shape, jnp.float32) * width * gain
    return jnp.minimum(jnp.maximum(entries, -bound), bound).astype(kind)


def setup_inputs(seed: int = 0) -> dict:
    keys = jax.random.split(jax.random.key(seed), 9)
    return {
        "features": bell_draw(keys[0], (N_DP, NODES, H), 1.0, 6.0, ((0, 8), (1, 64))),
        "send_order": jax.vmap(lambda own: jax.random.permutation(own, NODES_DEV))(jax.random.split(keys[1], N_DOM)).reshape((N_DOM, NODES_DEV)).astype(jnp.int32),
        "adj_count": draw_adj_count(jax.random.fold_in(keys[8], 71), 0),
        "adj_target": draw_adj_target(jax.random.fold_in(keys[8], 71), 0),
        "adj_vals": bell_draw(keys[4], (NBLOCKS, NB, 128, 128), 384 ** -0.5, 0.3125, ((0, 64),)),
        "w_edge": bell_draw(keys[5], (H, H), H ** -0.5, 0.375),
        "w_node": bell_draw(keys[6], (2 * H, H), (2 * H) ** -0.5, 0.25),
        "cotangent": bell_draw(keys[7], (N_DP, NODES, H), 1.0, 6.0, ((0, 8), (1, 64))),
    }


def dsilu(value):
    sig = jax.nn.sigmoid(value)
    return sig * (1.0 + value * (1.0 - sig))


def relay_index(send_order):
    offsets = (jnp.arange(N_DOM, dtype=jnp.int32) * NODES_DEV)[:, None, None]
    order = send_order.reshape(N_DOM, N_DOM, PER_PEER).astype(jnp.int32) + offsets
    return jnp.transpose(order, (1, 0, 2)).reshape(-1)


def slot_table(targets, counts):
    wins = jnp.arange(3 * BLK, dtype=jnp.int32)
    live = jnp.arange(NB, dtype=jnp.int32)[None, :] < counts[:, None]
    return ((targets[None, :, :] == wins[:, None, None]) & live[None]).astype(jnp.float32)


def reference(features, send_order, adj_count, adj_target, adj_vals, w_edge, w_node, cotangent):
    src = relay_index(send_order)
    vals_r = adj_vals.reshape(N_DOM, BLK, NB, 128, 128)
    tgt_r = adj_target.reshape(N_DOM, BLK, NB)
    cnt_r = adj_count.reshape(N_DOM, BLK)
    scale = 1.0 / (float(N_DP * NODES) ** 0.5)

    def window_fn(args):
        vq, tq, cq, mq = args
        contrib = jnp.einsum('csrk,ckh->csrh', vq.astype(jnp.float32), mq.astype(jnp.float32))
        table = slot_table(tq, cq)
        win = jnp.einsum('wcs,csrh->wrh', table, contrib, precision=lax.Precision.HIGHEST)
        return win.astype(jnp.bfloat16)

    def dmsg_fn(args):
        vq, tq, cq, gq = args
        table = slot_table(tq, cq)
        picked = jnp.einsum('wcs,wrh->csrh', table, gq.astype(jnp.float32), precision=lax.Precision.HIGHEST)
        out = jnp.einsum('csrk,csrh->ckh', vq.astype(jnp.float32), picked)
        return out.astype(jnp.bfloat16)

    def one_sample(args):
        xs, gs = args
        nodes = xs[src]
        pre_edge = jnp.dot(nodes, w_edge, preferred_element_type=jnp.float32)
        message = jax.nn.silu(pre_edge).astype(jnp.bfloat16)
        mr = message.reshape(N_DOM, BLK, 128, H)
        wins = lax.map(window_fn, (vals_r, tgt_r, cnt_r, mr)).astype(jnp.float32)
        agg = wins[:, BLK:2 * BLK] + jnp.roll(wins[:, :BLK], -1, 0) + jnp.roll(wins[:, 2 * BLK:], 1, 0)
        aggregate = agg.astype(jnp.bfloat16).reshape(NODES, H)
        joined = jnp.concatenate([nodes, aggregate], axis=1)
        pre_node = jnp.dot(joined, w_node, preferred_element_type=jnp.float32)
        node_out = (nodes.astype(jnp.float32) + jax.nn.silu(pre_node)).astype(jnp.bfloat16)
        gout = gs.astype(jnp.float32)
        d_node = (gout * dsilu(pre_node)).astype(jnp.bfloat16)
        back = jnp.dot(d_node, w_node.T, preferred_element_type=jnp.float32)
        d_nodes1 = gout + back[:, :H]
        d_agg = back[:, H:].astype(jnp.bfloat16).reshape(N_DOM, BLK, 128, H)
        window_g = jnp.concatenate([jnp.roll(d_agg, 1, 0), d_agg, jnp.roll(d_agg, -1, 0)], axis=1)
        d_message = lax.map(dmsg_fn, (vals_r, tgt_r, cnt_r, window_g)).reshape(NODES, H)
        d_edge = (d_message.astype(jnp.float32) * dsilu(pre_edge)).astype(jnp.bfloat16)
        d_nodes = (d_nodes1 + jnp.dot(d_edge, w_edge.T, preferred_element_type=jnp.float32)).astype(jnp.bfloat16)
        grad_x = jnp.zeros((NODES, H), jnp.bfloat16).at[src].set(d_nodes)
        g_edge = jnp.dot(nodes.T, d_edge, preferred_element_type=jnp.float32)
        g_node = jnp.dot(joined.T, d_node, preferred_element_type=jnp.float32)
        return node_out, grad_x, g_edge, g_node

    outs, grads_x, g_edges, g_nodes = lax.map(one_sample, (features, cotangent))
    return outs, grads_x, jnp.sum(g_edges, axis=0) * scale, jnp.sum(g_nodes, axis=0) * scale
```

```python
import functools
import math

import jax
import jax.numpy as jnp
from jax import lax
from jax.experimental import pallas as pl
from jax.experimental.pallas import tpu as pltpu
from jax.sharding import PartitionSpec as P

NDOM = 64
BF = jnp.bfloat16
F32 = jnp.float32
NT = (((1,), (1,)), ((), ()))
TN = (((0,), (0,)), ((), ()))


def dot(a, b):
    return jnp.dot(a, b, preferred_element_type=F32)


def sigmoid(v):
    return jax.nn.sigmoid(v)


def rows_of(b):
    return pl.ds(pl.multiple_of(b * 128, 128), 128)


def remote(src, dst, send, recv, where):
    return pltpu.make_async_remote_copy(
        src_ref=src,
        dst_ref=dst,
        send_sem=send,
        recv_sem=recv,
        device_id=where,
        device_id_type=pl.DeviceIdType.MESH,
    )


def layer_kernel(
    feat,
    order,
    cnt,
    tgt,
    vals_hbm,
    we_hbm,
    wn_hbm,
    cot_hbm,
    node_out,
    gx_out,
    g_out,
    vals,
    we,
    wn,
    cot,
    out_rows,
    nodes,
    pre_edge,
    message,
    adj,
    adj_t,
    perm_t,
    agg,
    pre_node,
    d_node,
    d_nodes1,
    rim_out,
    rim_in,
    dwin,
    d_edge,
    back_rows,
    returned,
    in_sems,
    relay_send,
    relay_recv,
    ret_send,
    ret_recv,
    halo_send,
    halo_recv,
):
    me = lax.axis_index("dom")
    row = me // 8
    prev = lax.rem(me + NDOM - 1, NDOM)
    nxt = lax.rem(me + 1, NDOM)

    barrier = pltpu.get_barrier_semaphore()

    @pl.loop(1, NDOM)
    def _(s):
        pl.semaphore_signal(
            barrier,
            inc=1,
            device_id={"dom": lax.rem(me + s, NDOM)},
            device_id_type=pl.DeviceIdType.MESH,
        )

    loads = [
        pltpu.make_async_copy(src, dst, in_sems.at[i])
        for i, (src, dst) in enumerate(
            [(vals_hbm, vals), (we_hbm, we), (wn_hbm, wn), (cot_hbm, cot)]
        )
    ]
    for copy in loads:
        copy.start()

    def send_group(src, dst, send, recv, b):
        for jj in range(8):
            k = b * 8 + jj

            @pl.when(k != me)
            def _():
                remote(src.at[k], dst.at[me], send, recv, {"dom": k}).start()

            @pl.when(k == me)
            def _():
                pltpu.make_async_copy(src.at[k], dst.at[me], recv).start()

    far_first = [4, 3, 5, 2, 6, 1, 7, 0]

    lanes = lax.broadcasted_iota(jnp.int32, (128, 1024), 1)
    for r, shift in enumerate(far_first):
        b = lax.rem(row + shift, 8)
        own = jnp.broadcast_to(order[pl.ds(b, 1), :], (128, 128)).T
        hot = jnp.where(jnp.concatenate([own] * 8, axis=1) == lanes, 1.0, 0.0)
        picked = dot(hot.astype(BF), feat[...]).astype(BF)
        out_rows[pl.ds(pl.multiple_of(b * 8, 8), 8)] = picked.reshape(8, 16, 256)
        if r == 0:
            pl.semaphore_wait(barrier, NDOM - 1)
        send_group(out_rows, nodes, relay_send, relay_recv.at[row], b)

    down = lax.broadcasted_iota(jnp.int32, (1024, 128), 0)
    for ib in range(8):
        mine = jnp.broadcast_to(order[ib : ib + 1, :], (1024, 128))
        perm_t[:, ib * 128 : (ib + 1) * 128] = jnp.where(mine == down, 1.0, 0.0).astype(BF)
    for copy in loads:
        copy.wait()

    @pl.loop(0, 8)
    def _(c):
        blocks = []
        for s in range(4):
            live = (cnt[c] > s).astype(jnp.int32).astype(F32)
            block = vals[c, s].astype(F32) * live
            blocks.append(block)
            adj_t[c, :, s * 128 : (s + 1) * 128] = block.T.astype(BF)
        for w in range(12):
            total = None
            for s in range(4):
                hit = (tgt[c, s] == w + 6).astype(jnp.int32).astype(F32)
                term = blocks[s] * hit
                total = term if total is None else total + term
            adj[w * 128 : (w + 1) * 128, rows_of(c)] = total.astype(BF)

    for shift in reversed(far_first):
        b = lax.rem(row + shift, 8)
        group = nodes.at[pl.ds(pl.multiple_of(b * 8, 8), 8)]
        pltpu.make_async_copy(group, group, relay_recv.at[b]).wait()
        rows = group[...].reshape(128, 256)
        v = dot(rows, we[...])
        pre_edge[rows_of(b), :] = v
        message[rows_of(b), :] = (v * sigmoid(v)).astype(BF)

    rim_out[0] = dot(adj[0:256, :], message[...]).astype(BF)
    to_prev = remote(rim_out.at[0], rim_in.at[0], halo_send.at[0], halo_recv.at[0], {"dom": prev})
    to_prev.start()
    rim_out[1] = dot(adj[1280:1536, :], message[...]).astype(BF)
    to_next = remote(rim_out.at[1], rim_in.at[1], halo_send.at[1], halo_recv.at[1], {"dom": nxt})
    to_next.start()

    def flat_nodes(lo, n):
        return nodes[lo // 16 : (lo + n) // 16].reshape(n, 256)

    def node_step(lo, n):
        here = slice(lo, lo + n)
        own = flat_nodes(lo, n)
        v = pre_node[here, :] + dot(agg[here, :], wn[256:512, :])
        sig = sigmoid(v)
        node_out[here, :] = (own.astype(F32) + v * sig).astype(BF)
        g = cot[here, :].astype(F32)
        d = (g * (sig * (1.0 + v * (1.0 - sig)))).astype(BF)
        d_node[here, :] = d
        back = lax.dot_general(d, wn[...], NT, preferred_element_type=F32)
        d_nodes1[here, :] = g + back[:, :256]
        dwin[2 + lo // 128 : 2 + (lo + n) // 128] = back[:, 256:].astype(BF).reshape(n // 128, 128, 256)

    for lo in range(0, 1024, 256):
        pre_node[lo : lo + 256, :] = dot(flat_nodes(lo, 256), wn[0:256, :])
    for lo in (256, 512, 0, 768):
        agg[lo : lo + 256, :] = dot(adj[lo + 256 : lo + 512, :], message[...]).astype(BF)
    node_step(256, 512)

    to_prev.wait_recv()
    agg[768:1024, :] = (agg[768:1024, :].astype(F32) + rim_in[0].astype(F32)).astype(BF)
    node_step(768, 256)
    give_next = remote(dwin.at[8:10], dwin.at[0:2], halo_send.at[2], halo_recv.at[2], {"dom": nxt})
    give_next.start()
    to_next.wait_recv()
    agg[0:256, :] = (agg[0:256, :].astype(F32) + rim_in[1].astype(F32)).astype(BF)
    node_step(0, 256)
    give_prev = remote(dwin.at[2:4], dwin.at[10:12], halo_send.at[3], halo_recv.at[3], {"dom": prev})
    give_prev.start()

    g_out[256:512, :] = lax.dot_general(flat_nodes(0, 1024), d_node[...], TN, preferred_element_type=F32)
    g_out[512:768, :] = lax.dot_general(agg[...], d_node[...], TN, preferred_element_type=F32)
    for lo in range(0, 1024, 256):
        v = pre_edge[lo : lo + 256, :]
        sig = sigmoid(v)
        pre_edge[lo : lo + 256, :] = sig * (1.0 + v * (1.0 - sig))

    give_next.wait_recv()
    give_prev.wait_recv()
    for shift in far_first:
        c = lax.rem(row + shift, 8)
        gathered = jnp.concatenate([dwin[jnp.clip(tgt[c, s] - 6, 0, 11)] for s in range(4)], axis=0)
        dm = dot(adj_t[c], gathered).astype(BF)
        de = (dm.astype(F32) * pre_edge[rows_of(c), :]).astype(BF)
        d_edge[rows_of(c), :] = de
        dn = d_nodes1[rows_of(c), :] + lax.dot_general(de, we[...], NT, preferred_element_type=F32)
        back_rows[pl.ds(pl.multiple_of(c * 8, 8), 8)] = dn.astype(BF).reshape(8, 16, 256)
        send_group(back_rows, returned, ret_send, ret_recv, c)

    g_out[0:256, :] = lax.dot_general(flat_nodes(0, 1024), d_edge[...], TN, preferred_element_type=F32)

    pltpu.make_async_copy(returned, returned, ret_recv).wait()
    rows = returned[...].reshape(1024, 256)
    for lo in range(0, 1024, 256):
        gx_out[lo : lo + 256, :] = dot(perm_t[lo : lo + 256, :], rows).astype(BF)

    for copy in (to_prev, to_next, give_next, give_prev):
        copy.wait_send()
    others = pl.ds(0, NDOM - 1)
    for src, dst, send, recv in (
        (out_rows, nodes, relay_send, relay_recv.at[0]),
        (back_rows, returned, ret_send, ret_recv),
    ):
        remote(src.at[others], dst.at[others], send, recv, {"dom": nxt}).wait_send()


def shards(features, send_order, adj_count, adj_target, adj_vals, w_edge, w_node, cotangent):
    vmem = pl.BlockSpec(memory_space=pltpu.VMEM)
    smem = pl.BlockSpec(memory_space=pltpu.SMEM)
    hbm = pl.BlockSpec(memory_space=pl.ANY)
    V = pltpu.VMEM
    dma = pltpu.SemaphoreType.DMA
    node_out, gx, g = pl.pallas_call(
        layer_kernel,
        out_shape=(
            jax.ShapeDtypeStruct((1024, 256), BF),
            jax.ShapeDtypeStruct((1024, 256), BF),
            jax.ShapeDtypeStruct((768, 256), F32),
        ),
        in_specs=[vmem, vmem, smem, smem, hbm, hbm, hbm, hbm],
        out_specs=(vmem, vmem, vmem),
        scratch_shapes=[
            V((8, 4, 128, 128), BF),
            V((256, 256), BF),
            V((512, 256), BF),
            V((1024, 256), BF),
            V((64, 16, 256), BF),
            V((64, 16, 256), BF),
            V((1024, 256), F32),
            V((1024, 256), BF),
            V((1536, 1024), BF),
            V((8, 128, 512), BF),
            V((1024, 1024), BF),
            V((1024, 256), BF),
            V((1024, 256), F32),
            V((1024, 256), BF),
            V((1024, 256), F32),
            V((2, 256, 256), BF),
            V((2, 256, 256), BF),
            V((12, 128, 256), BF),
            V((1024, 256), BF),
            V((64, 16, 256), BF),
            V((64, 16, 256), BF),
            dma((4,)),
            dma(()),
            dma((8,)),
            dma(()),
            dma(()),
            dma((4,)),
            dma((4,)),
        ],
        compiler_params=pltpu.CompilerParams(
            collective_id=0, has_side_effects=True, vmem_limit_bytes=48 << 20
        ),
        name="layer",
    )(
        features[0],
        send_order.reshape(8, 128),
        adj_count,
        adj_target,
        adj_vals,
        w_edge,
        w_node,
        cotangent[0],
    )
    scale = 1.0 / math.sqrt(float(lax.axis_size("dp") * features.shape[1] * lax.axis_size("dom")))
    g = lax.psum(g, ("dp", "dom")) * scale
    return node_out[None], gx[None], g[:256], g[256:]


def solution(mesh):
    in_specs = (
        P("dp", "dom", None),
        P("dom", None),
        P("dom"),
        P("dom", None),
        P("dom", None, None, None),
        P(),
        P(),
        P("dp", "dom", None),
    )
    out_specs = (P("dp", "dom", None), P("dp", "dom", None), P(), P())
    return jax.shard_map(shards, mesh=mesh, in_specs=in_specs, out_specs=out_specs, check_vma=False)
```

```python
import functools
import math

import jax
import jax.numpy as jnp
from jax import lax
from jax.experimental import pallas as pl
from jax.experimental.pallas import tpu as pltpu
from jax.sharding import PartitionSpec as P

NDOM = 64
BF = jnp.bfloat16
F32 = jnp.float32
NT = (((1,), (1,)), ((), ()))
TN = (((0,), (0,)), ((), ()))


def dot(a, b):
    return jnp.dot(a, b, preferred_element_type=F32)


def sigmoid(v):
    return jax.nn.sigmoid(v)


def rows_of(b):
    return pl.ds(pl.multiple_of(b * 128, 128), 128)


def remote(src, dst, send, recv, where):
    return pltpu.make_async_remote_copy(
        src_ref=src,
        dst_ref=dst,
        send_sem=send,
        recv_sem=recv,
        device_id=where,
        device_id_type=pl.DeviceIdType.MESH,
    )


def layer_kernel(
    scale,
    feat_hbm,
    order,
    cnt,
    tgt,
    vals_hbm,
    we_hbm,
    wn_hbm,
    cot_hbm,
    node_out,
    gx_out,
    ge_out,
    gn_out,
    feat,
    vals,
    we,
    wn,
    cot,
    out_rows,
    nodes,
    pre_edge,
    message,
    adj,
    adj_t,
    perm_t,
    agg,
    pre_node,
    d_node,
    d_nodes1,
    rim_out,
    rim_in,
    dwin,
    d_edge,
    back_rows,
    returned,
    part_n,
    part_e,
    got_n,
    got_e,
    sum_y,
    sum_x,
    whole,
    in_sems,
    relay_send,
    relay_recv,
    ret_send,
    ret_recv,
    halo_send,
    halo_recv,
    grad_send,
    grad_recv,
):
    me = lax.axis_index("dom")
    plane = lax.axis_index("dp")
    core = lax.rem(me, 2)
    col = lax.rem(me // 2, 4)
    part = plane * 2 + core
    parts = range(1, 16)

    def member(step):
        m = lax.rem(part + step, 16)
        return m, {"dp": m // 2, "dom": me - core + lax.rem(m, 2)}
    row = me // 8
    prev = lax.rem(me + NDOM - 1, NDOM)
    nxt = lax.rem(me + 1, NDOM)

    barrier = pltpu.get_barrier_semaphore()

    @pl.loop(1, NDOM)
    def _(s):
        pl.semaphore_signal(
            barrier,
            inc=1,
            device_id={"dom": lax.rem(me + s, NDOM)},
            device_id_type=pl.DeviceIdType.MESH,
        )

    for step in range(1, 8):
        for other in range(2):
            pl.semaphore_signal(
                barrier,
                inc=1,
                device_id={"dp": lax.rem(plane + step, 8), "dom": me - core + other},
                device_id_type=pl.DeviceIdType.MESH,
            )

    loads = [
        pltpu.make_async_copy(src, dst, in_sems.at[i])
        for i, (src, dst) in enumerate(
            [(feat_hbm, feat), (vals_hbm, vals), (we_hbm, we), (wn_hbm, wn), (cot_hbm, cot)]
        )
    ]
    for copy in loads:
        copy.start()

    def send_group(src, dst, send, recv, b):
        for jj in range(8):
            k = b * 8 + jj

            @pl.when(k != me)
            def _():
                remote(src.at[k], dst.at[me], send, recv, {"dom": k}).start()

            @pl.when(k == me)
            def _():
                pltpu.make_async_copy(src.at[k], dst.at[me], recv).start()

    loads[0].wait()
    far_first = [4, 3, 5, 2, 6, 1, 7, 0]

    lanes = lax.broadcasted_iota(jnp.int32, (128, 1024), 1)
    for r, shift in enumerate(far_first):
        b = lax.rem(row + shift, 8)
        own = jnp.broadcast_to(order[pl.ds(b, 1), :], (128, 128)).T
        hot = jnp.where(jnp.concatenate([own] * 8, axis=1) == lanes, 1.0, 0.0)
        picked = dot(hot.astype(BF), feat[...]).astype(BF)
        out_rows[pl.ds(pl.multiple_of(b * 8, 8), 8)] = picked.reshape(8, 16, 256)
        if r == 0:
            pl.semaphore_wait(barrier, NDOM - 1 + 14)
        send_group(out_rows, nodes, relay_send, relay_recv.at[row], b)

    down = lax.broadcasted_iota(jnp.int32, (1024, 128), 0)
    for ib in range(8):
        mine = jnp.broadcast_to(order[ib : ib + 1, :], (1024, 128))
        perm_t[:, ib * 128 : (ib + 1) * 128] = jnp.where(mine == down, 1.0, 0.0).astype(BF)
    for copy in loads[1:]:
        copy.wait()

    @pl.loop(0, 8)
    def _(c):
        blocks = []
        for s in range(4):
            live = (cnt[c] > s).astype(jnp.int32).astype(F32)
            block = vals[c, s].astype(F32) * live
            blocks.append(block)
            adj_t[c, :, s * 128 : (s + 1) * 128] = block.T.astype(BF)
        for w in range(12):
            total = None
            for s in range(4):
                hit = (tgt[s, c] == w + 6).astype(jnp.int32).astype(F32)
                term = blocks[s] * hit
                total = term if total is None else total + term
            adj[w * 128 : (w + 1) * 128, rows_of(c)] = total.astype(BF)

    for shift in reversed(far_first):
        b = lax.rem(row + shift, 8)
        group = nodes.at[pl.ds(pl.multiple_of(b * 8, 8), 8)]
        pltpu.make_async_copy(group, group, relay_recv.at[b]).wait()
        rows = group[...].reshape(128, 256)
        v = dot(rows, we[...])
        pre_edge[rows_of(b), :] = v
        message[rows_of(b), :] = (v * sigmoid(v)).astype(BF)

    rim_out[0] = dot(adj[0:256, :], message[...]).astype(BF)
    to_prev = remote(rim_out.at[0], rim_in.at[0], halo_send.at[0], halo_recv.at[0], {"dom": prev})
    to_prev.start()
    rim_out[1] = dot(adj[1280:1536, :], message[...]).astype(BF)
    to_next = remote(rim_out.at[1], rim_in.at[1], halo_send.at[1], halo_recv.at[1], {"dom": nxt})
    to_next.start()

    def flat_nodes(lo, n):
        return nodes[lo // 16 : (lo + n) // 16].reshape(n, 256)

    def node_step(lo, n):
        here = slice(lo, lo + n)
        own = flat_nodes(lo, n)
        v = pre_node[here, :] + dot(agg[here, :], wn[256:512, :])
        sig = sigmoid(v)
        node_out[here, :] = (own.astype(F32) + v * sig).astype(BF)
        g = cot[here, :].astype(F32)
        d = (g * (sig * (1.0 + v * (1.0 - sig)))).astype(BF)
        d_node[here, :] = d
        back = lax.dot_general(d, wn[...], NT, preferred_element_type=F32)
        d_nodes1[here, :] = g + back[:, :256]
        dwin[2 + lo // 128 : 2 + (lo + n) // 128] = back[:, 256:].astype(BF).reshape(n // 128, 128, 256)

    for lo in range(0, 1024, 256):
        pre_node[lo : lo + 256, :] = dot(flat_nodes(lo, 256), wn[0:256, :])
    for lo in (256, 512, 0, 768):
        agg[lo : lo + 256, :] = dot(adj[lo + 256 : lo + 512, :], message[...]).astype(BF)
    node_step(256, 512)

    to_prev.wait_recv()
    agg[768:1024, :] = (agg[768:1024, :].astype(F32) + rim_in[0].astype(F32)).astype(BF)
    node_step(768, 256)
    give_next = remote(dwin.at[8:10], dwin.at[0:2], halo_send.at[2], halo_recv.at[2], {"dom": nxt})
    give_next.start()
    to_next.wait_recv()
    agg[0:256, :] = (agg[0:256, :].astype(F32) + rim_in[1].astype(F32)).astype(BF)
    node_step(0, 256)
    give_prev = remote(dwin.at[2:4], dwin.at[10:12], halo_send.at[3], halo_recv.at[3], {"dom": prev})
    give_prev.start()

    top = lax.dot_general(flat_nodes(0, 1024), d_node[...], TN, preferred_element_type=F32)
    low = lax.dot_general(agg[...], d_node[...], TN, preferred_element_type=F32)
    part_n[0:8] = top.astype(BF).reshape(8, 32, 256)
    part_n[8:16] = low.astype(BF).reshape(8, 32, 256)
    got_n[part] = part_n[part]
    for step in parts:
        m, where = member(step)
        remote(part_n.at[m], got_n.at[part], grad_send.at[0], grad_recv.at[0], where).start()
    for lo in range(0, 1024, 256):
        v = pre_edge[lo : lo + 256, :]
        sig = sigmoid(v)
        pre_edge[lo : lo + 256, :] = sig * (1.0 + v * (1.0 - sig))

    give_next.wait_recv()
    give_prev.wait_recv()
    for c in range(8):
        here = slice(c * 128, (c + 1) * 128)
        gathered = jnp.concatenate([dwin[jnp.clip(tgt[s, c] - 6, 0, 11)] for s in range(4)], axis=0)
        dm = dot(adj_t[c], gathered).astype(BF)
        d_edge[here, :] = (dm.astype(F32) * pre_edge[here, :]).astype(BF)

    edge = lax.dot_general(flat_nodes(0, 1024), d_edge[...], TN, preferred_element_type=F32)
    part_e[...] = edge.astype(BF).reshape(16, 16, 256)
    got_e[part] = part_e[part]
    for step in parts:
        m, where = member(step)
        remote(part_e.at[m], got_e.at[part], grad_send.at[1], grad_recv.at[1], where).start()

    for shift in far_first:
        c = lax.rem(row + shift, 8)
        de = d_edge[rows_of(c), :]
        dn = d_nodes1[rows_of(c), :] + lax.dot_general(de, we[...], NT, preferred_element_type=F32)
        back_rows[pl.ds(pl.multiple_of(c * 8, 8), 8)] = dn.astype(BF).reshape(8, 16, 256)
        send_group(back_rows, returned, ret_send, ret_recv, c)

    def counted(src, dst, sems, n):
        many = pl.ds(0, n)
        return remote(src.at[many], dst.at[many], grad_send.at[sems], grad_recv.at[sems], {"dom": nxt})

    def added(ref):
        total = ref[0].astype(F32)
        for i in range(1, ref.shape[0]):
            total = total + ref[i].astype(F32)
        return total

    counted(part_n, got_n, 0, 15).wait_recv()
    counted(part_e, got_e, 1, 15).wait_recv()
    sum_y[row, 0:16] = added(got_e).astype(BF)
    sum_y[row, 16:48] = added(got_n).astype(BF)
    for step in range(1, 8):
        other = lax.rem(row + step, 8)
        mine = sum_y.at[row]
        remote(mine, mine, grad_send.at[2], grad_recv.at[2], {"dom": other * 8 + lax.rem(me, 8)}).start()
    counted(sum_y, sum_y, 2, 7).wait_recv()
    sum_x[col] = added(sum_y).astype(BF)
    for step in range(1, 4):
        other = lax.rem(col + step, 4)
        mine = sum_x.at[col]
        remote(mine, mine, grad_send.at[3], grad_recv.at[3], {"dom": row * 8 + other * 2 + core}).start()
    counted(sum_x, sum_x, 3, 3).wait_recv()
    whole[part] = (added(sum_x) * scale).astype(BF)
    for step in parts:
        m, where = member(step)
        mine = whole.at[part]
        remote(mine, mine, grad_send.at[4], grad_recv.at[4], where).start()

    pltpu.make_async_copy(returned, returned, ret_recv).wait()
    rows = returned[...].reshape(1024, 256)
    for lo in range(0, 1024, 256):
        gx_out[lo : lo + 256, :] = dot(perm_t[lo : lo + 256, :], rows).astype(BF)

    counted(whole, whole, 4, 15).wait_recv()
    ge_out[...] = whole[:, 0:16].astype(F32).reshape(256, 256)
    gn_out[...] = whole[:, 16:48].astype(F32).reshape(512, 256)

    counted(part_n, got_n, 0, 15).wait_send()
    counted(part_e, got_e, 1, 15).wait_send()
    counted(sum_y, sum_y, 2, 7).wait_send()
    counted(sum_x, sum_x, 3, 3).wait_send()
    counted(whole, whole, 4, 15).wait_send()
    for copy in (to_prev, to_next, give_next, give_prev):
        copy.wait_send()
    others = pl.ds(0, NDOM - 1)
    for src, dst, send, recv in (
        (out_rows, nodes, relay_send, relay_recv.at[0]),
        (back_rows, returned, ret_send, ret_recv),
    ):
        remote(src.at[others], dst.at[others], send, recv, {"dom": nxt}).wait_send()


def shards(features, send_order, adj_count, adj_target, adj_vals, w_edge, w_node, cotangent):
    vmem = pl.BlockSpec(memory_space=pltpu.VMEM)
    smem = pl.BlockSpec(memory_space=pltpu.SMEM)
    hbm = pl.BlockSpec(memory_space=pl.ANY)
    V = pltpu.VMEM
    dma = pltpu.SemaphoreType.DMA
    scale = 1.0 / math.sqrt(float(lax.axis_size("dp") * features.shape[1] * lax.axis_size("dom")))
    node_out, gx, ge, gn = pl.pallas_call(
        functools.partial(layer_kernel, scale),
        out_shape=(
            jax.ShapeDtypeStruct((1024, 256), BF),
            jax.ShapeDtypeStruct((1024, 256), BF),
            jax.ShapeDtypeStruct((256, 256), F32),
            jax.ShapeDtypeStruct((512, 256), F32),
        ),
        in_specs=[hbm, vmem, smem, smem, hbm, hbm, hbm, hbm],
        out_specs=(vmem, vmem, vmem, vmem),
        scratch_shapes=[
            V((1024, 256), BF),
            V((8, 4, 128, 128), BF),
            V((256, 256), BF),
            V((512, 256), BF),
            V((1024, 256), BF),
            V((64, 16, 256), BF),
            V((64, 16, 256), BF),
            V((1024, 256), F32),
            V((1024, 256), BF),
            V((1536, 1024), BF),
            V((8, 128, 512), BF),
            V((1024, 1024), BF),
            V((1024, 256), BF),
            V((1024, 256), F32),
            V((1024, 256), BF),
            V((1024, 256), F32),
            V((2, 256, 256), BF),
            V((2, 256, 256), BF),
            V((12, 128, 256), BF),
            V((1024, 256), BF),
            V((64, 16, 256), BF),
            V((64, 16, 256), BF),
            V((16, 32, 256), BF),
            V((16, 16, 256), BF),
            V((16, 32, 256), BF),
            V((16, 16, 256), BF),
            V((8, 48, 256), BF),
            V((4, 48, 256), BF),
            V((16, 48, 256), BF),
            dma((5,)),
            dma(()),
            dma((8,)),
            dma(()),
            dma(()),
            dma((4,)),
            dma((4,)),
            dma((5,)),
            dma((5,)),
        ],
        compiler_params=pltpu.CompilerParams(
            collective_id=0, has_side_effects=True, vmem_limit_bytes=60 << 20
        ),
        name="layer",
    )(
        features[0],
        send_order.reshape(8, 128),
        adj_count,
        adj_target.T,
        adj_vals,
        w_edge,
        w_node,
        cotangent[0],
    )
    return node_out[None], gx[None], ge, gn


def solution(mesh):
    in_specs = (
        P("dp", "dom", None),
        P("dom", None),
        P("dom"),
        P("dom", None),
        P("dom", None, None, None),
        P(),
        P(),
        P("dp", "dom", None),
    )
    out_specs = (P("dp", "dom", None), P("dp", "dom", None), P(), P())
    return jax.shard_map(shards, mesh=mesh, in_specs=in_specs, out_specs=out_specs, check_vma=False)
```

```python
import functools
import math

import jax
import jax.numpy as jnp
from jax import lax
from jax.experimental import pallas as pl
from jax.experimental.pallas import tpu as pltpu
from jax.sharding import PartitionSpec as P

NDOM = 64
BF = jnp.bfloat16
F32 = jnp.float32
NT = (((1,), (1,)), ((), ()))
TN = (((0,), (0,)), ((), ()))


def dot(a, b):
    return jnp.dot(a, b, preferred_element_type=F32)


def sigmoid(v):
    return jax.nn.sigmoid(v)


def rows_of(b):
    return pl.ds(pl.multiple_of(b * 128, 128), 128)


def remote(src, dst, send, recv, where):
    return pltpu.make_async_remote_copy(
        src_ref=src,
        dst_ref=dst,
        send_sem=send,
        recv_sem=recv,
        device_id=where,
        device_id_type=pl.DeviceIdType.MESH,
    )


def layer_kernel(
    scale,
    feat_hbm,
    order,
    cnt,
    tgt,
    vals_hbm,
    we_hbm,
    wn_hbm,
    cot_hbm,
    node_hbm,
    gx_hbm,
    ge_hbm,
    gn_hbm,
    feat,
    vals,
    we,
    wn,
    cot,
    out_rows,
    nodes,
    pre_edge,
    message,
    adj,
    adj_t,
    perm_t,
    agg,
    pre_node,
    d_node,
    d_nodes1,
    rim_out,
    rim_in,
    dwin,
    d_edge,
    back_rows,
    returned,
    node_out,
    gx_out,
    part_n,
    part_e,
    give_n,
    give_e,
    half_n,
    half_e,
    send_n,
    send_e,
    got_n,
    got_e,
    sum_yn,
    sum_ye,
    sum_xn,
    sum_xe,
    whole_n,
    whole_e,
    in_sems,
    relay_send,
    relay_recv,
    ret_send,
    ret_recv,
    halo_send,
    halo_recv,
    grad_send,
    grad_recv,
    out_sems,
):
    me = lax.axis_index("dom")
    plane = lax.axis_index("dp")
    core = lax.rem(me, 2)
    row = me // 8
    col = lax.rem(me // 2, 4)
    sibling = {"dom": me + 1 - 2 * core}
    prev = lax.rem(me + NDOM - 1, NDOM)
    nxt = lax.rem(me + 1, NDOM)

    barrier = pltpu.get_barrier_semaphore()

    @pl.loop(1, NDOM)
    def _(s):
        pl.semaphore_signal(
            barrier,
            inc=1,
            device_id={"dom": lax.rem(me + s, NDOM)},
            device_id_type=pl.DeviceIdType.MESH,
        )

    for step in range(1, 8):
        pl.semaphore_signal(
            barrier,
            inc=1,
            device_id={"dp": lax.rem(plane + step, 8)},
            device_id_type=pl.DeviceIdType.MESH,
        )

    loads = [
        pltpu.make_async_copy(src, dst, in_sems.at[i])
        for i, (src, dst) in enumerate(
            [(feat_hbm, feat), (vals_hbm, vals), (we_hbm, we), (wn_hbm, wn), (cot_hbm, cot)]
        )
    ]
    for copy in loads:
        copy.start()

    def send_group(src, dst, send, recv, b, shift):
        for jj in range(8):
            k = b * 8 + jj
            if shift:
                remote(src.at[k], dst.at[me], send, recv, {"dom": k}).start()
                continue

            @pl.when(k != me)
            def _():
                remote(src.at[k], dst.at[me], send, recv, {"dom": k}).start()

            @pl.when(k == me)
            def _():
                pltpu.make_async_copy(src.at[k], dst.at[me], recv).start()

    loads[0].wait()
    far_first = [4, 3, 5, 2, 6, 1, 7, 0]

    lanes = lax.broadcasted_iota(jnp.int32, (128, 1024), 1)
    for r, shift in enumerate(far_first):
        b = lax.rem(row + shift, 8)
        own = jnp.broadcast_to(order[pl.ds(b, 1), :], (128, 128)).T
        hot = jnp.where(jnp.concatenate([own] * 8, axis=1) == lanes, 1.0, 0.0)
        picked = dot(hot.astype(BF), feat[...]).astype(BF)
        out_rows[pl.ds(pl.multiple_of(b * 8, 8), 8)] = picked.reshape(8, 16, 256)
        if r == 0:
            pl.semaphore_wait(barrier, NDOM - 1 + 7)
        send_group(out_rows, nodes, relay_send, relay_recv.at[row], b, shift)

    down = lax.broadcasted_iota(jnp.int32, (1024, 128), 0)
    for ib in range(8):
        mine = jnp.broadcast_to(order[ib : ib + 1, :], (1024, 128))
        perm_t[:, ib * 128 : (ib + 1) * 128] = jnp.where(mine == down, 1.0, 0.0).astype(BF)
    for copy in loads[1:]:
        copy.wait()

    @pl.loop(0, 8)
    def _(c):
        blocks = []
        for s in range(4):
            live = (cnt[c] > s).astype(jnp.int32).astype(F32)
            block = vals[c, s].astype(F32) * live
            blocks.append(block)
            adj_t[c, :, s * 128 : (s + 1) * 128] = block.T.astype(BF)
        for w in range(12):
            total = None
            for s in range(4):
                hit = (tgt[s, c] == w + 6).astype(jnp.int32).astype(F32)
                term = blocks[s] * hit
                total = term if total is None else total + term
            adj[w * 128 : (w + 1) * 128, rows_of(c)] = total.astype(BF)

    for shift in reversed(far_first):
        b = lax.rem(row + shift, 8)
        group = nodes.at[pl.ds(pl.multiple_of(b * 8, 8), 8)]
        pltpu.make_async_copy(group, group, relay_recv.at[b]).wait()
        rows = group[...].reshape(128, 256)
        v = dot(rows, we[...])
        pre_edge[rows_of(b), :] = v
        message[rows_of(b), :] = (v * sigmoid(v)).astype(BF)

    rim_out[0] = dot(adj[0:256, :], message[...]).astype(BF)
    to_prev = remote(rim_out.at[0], rim_in.at[0], halo_send.at[0], halo_recv.at[0], {"dom": prev})
    to_prev.start()
    rim_out[1] = dot(adj[1280:1536, :], message[...]).astype(BF)
    to_next = remote(rim_out.at[1], rim_in.at[1], halo_send.at[1], halo_recv.at[1], {"dom": nxt})
    to_next.start()

    def flat_nodes(lo, n):
        return nodes[lo // 16 : (lo + n) // 16].reshape(n, 256)

    def node_step(lo, n):
        here = slice(lo, lo + n)
        own = flat_nodes(lo, n)
        v = pre_node[here, :] + dot(agg[here, :], wn[256:512, :])
        sig = sigmoid(v)
        node_out[here, :] = (own.astype(F32) + v * sig).astype(BF)
        g = cot[here, :].astype(F32)
        d = (g * (sig * (1.0 + v * (1.0 - sig)))).astype(BF)
        d_node[here, :] = d
        back = lax.dot_general(d, wn[...], NT, preferred_element_type=F32)
        d_nodes1[here, :] = g + back[:, :256]
        dwin[2 + lo // 128 : 2 + (lo + n) // 128] = back[:, 256:].astype(BF).reshape(n // 128, 128, 256)

    for lo in range(0, 1024, 256):
        pre_node[lo : lo + 256, :] = dot(flat_nodes(lo, 256), wn[0:256, :])
    for lo in (256, 512, 0, 768):
        agg[lo : lo + 256, :] = dot(adj[lo + 256 : lo + 512, :], message[...]).astype(BF)
    node_step(256, 512)

    to_prev.wait_recv()
    agg[768:1024, :] = (agg[768:1024, :].astype(F32) + rim_in[0].astype(F32)).astype(BF)
    node_step(768, 256)
    give_next = remote(dwin.at[8:10], dwin.at[0:2], halo_send.at[2], halo_recv.at[2], {"dom": nxt})
    give_next.start()
    to_next.wait_recv()
    agg[0:256, :] = (agg[0:256, :].astype(F32) + rim_in[1].astype(F32)).astype(BF)
    node_step(0, 256)
    give_prev = remote(dwin.at[2:4], dwin.at[10:12], halo_send.at[3], halo_recv.at[3], {"dom": prev})
    give_prev.start()

    outs = [pltpu.make_async_copy(node_out, node_hbm, out_sems.at[0])]
    outs[0].start()

    def counted(src, dst, i, n):
        many = pl.ds(0, n)
        return remote(src.at[many], dst.at[many], grad_send.at[i], grad_recv.at[i], sibling)

    def swap_halves(total, part, give, half, i):
        part[...] = total.reshape(16, -1, 256)
        other = pl.multiple_of((1 - core) * 8, 8)
        give[...] = part[pl.ds(other, 8)].astype(BF)
        copy = remote(give, half, grad_send.at[i], grad_recv.at[i], sibling)
        copy.start()
        return copy

    def over_planes(copy, part, half, send, got, i):
        copy.wait_recv()
        mine = part[pl.ds(pl.multiple_of(core * 8, 8), 8)]
        send[...] = (mine + half[...].astype(F32)).astype(BF)
        got[plane] = send[plane]
        for step in range(1, 8):
            z = lax.rem(plane + step, 8)
            remote(send.at[z], got.at[plane], grad_send.at[i], grad_recv.at[i], {"dp": z}).start()

    def added(ref):
        total = ref[0].astype(F32)
        for i in range(1, ref.shape[0]):
            total = total + ref[i].astype(F32)
        return total

    def over_y(send, got, ring, i, j):
        counted(send, got, i, 7).wait_recv()
        ring[row] = added(got).astype(BF)
        mine = ring.at[row]
        for step in range(1, 8):
            k = lax.rem(row + step, 8) * 8 + lax.rem(me, 8)
            remote(mine, mine, grad_send.at[j], grad_recv.at[j], {"dom": k}).start()

    def over_x(ring_y, ring, i, j):
        counted(ring_y, ring_y, i, 7).wait_recv()
        ring[col] = added(ring_y).astype(BF)
        mine = ring.at[col]
        for step in range(1, 4):
            k = row * 8 + lax.rem(col + step, 4) * 2 + core
            remote(mine, mine, grad_send.at[j], grad_recv.at[j], {"dom": k}).start()

    def spread_planes(ring_x, whole, i, j):
        counted(ring_x, ring_x, i, 3).wait_recv()
        mine = whole.at[core * 8 + plane]
        mine[...] = (added(ring_x) * scale).astype(BF)
        for step in range(1, 8):
            remote(mine, mine, grad_send.at[j], grad_recv.at[j], {"dp": lax.rem(plane + step, 8)}).start()

    def spread_cores(whole, i, j):
        counted(whole, whole, i, 7).wait_recv()
        mine = whole.at[pl.ds(pl.multiple_of(core * 8, 8), 8)]
        copy = remote(mine, mine, grad_send.at[j], grad_recv.at[j], sibling)
        copy.start()
        return copy

    top = lax.dot_general(flat_nodes(0, 1024), d_node[...], TN, preferred_element_type=F32)
    low = lax.dot_general(agg[...], d_node[...], TN, preferred_element_type=F32)
    swap_n = swap_halves(jnp.concatenate([top, low], axis=0), part_n, give_n, half_n, 0)
    for lo in range(0, 1024, 256):
        v = pre_edge[lo : lo + 256, :]
        sig = sigmoid(v)
        pre_edge[lo : lo + 256, :] = sig * (1.0 + v * (1.0 - sig))

    give_next.wait_recv()
    give_prev.wait_recv()
    for c in range(8):
        here = slice(c * 128, (c + 1) * 128)
        gathered = jnp.concatenate([dwin[jnp.clip(tgt[s, c] - 6, 0, 11)] for s in range(4)], axis=0)
        dm = dot(adj_t[c], gathered).astype(BF)
        d_edge[here, :] = (dm.astype(F32) * pre_edge[here, :]).astype(BF)

    over_planes(swap_n, part_n, half_n, send_n, got_n, 1)
    edge = lax.dot_general(flat_nodes(0, 1024), d_edge[...], TN, preferred_element_type=F32)
    swap_e = swap_halves(edge, part_e, give_e, half_e, 2)

    def send_back(shifts):
        for shift in shifts:
            c = lax.rem(row + shift, 8)
            de = d_edge[rows_of(c), :]
            dn = d_nodes1[rows_of(c), :] + lax.dot_general(de, we[...], NT, preferred_element_type=F32)
            back_rows[pl.ds(pl.multiple_of(c * 8, 8), 8)] = dn.astype(BF).reshape(8, 16, 256)
            send_group(back_rows, returned, ret_send, ret_recv, c, shift)

    send_back([4])
    over_planes(swap_e, part_e, half_e, send_e, got_e, 3)
    send_back([5])
    over_y(send_n, got_n, sum_yn, 1, 4)
    over_y(send_e, got_e, sum_ye, 3, 5)
    send_back([3, 6])
    over_x(sum_yn, sum_xn, 4, 6)
    over_x(sum_ye, sum_xe, 5, 7)
    send_back([2, 7, 1, 0])
    spread_planes(sum_xn, whole_n, 6, 8)
    spread_planes(sum_xe, whole_e, 7, 9)
    last_n = spread_cores(whole_n, 8, 10)

    pltpu.make_async_copy(returned, returned, ret_recv).wait()
    rows = returned[...].reshape(1024, 256)
    for i, lo in enumerate(range(0, 1024, 256)):
        gx_out[lo : lo + 256, :] = dot(perm_t[lo : lo + 256, :], rows).astype(BF)
        here = pl.ds(lo, 256)
        outs.append(pltpu.make_async_copy(gx_out.at[here], gx_hbm.at[here], out_sems.at[1 + i]))
        outs[-1].start()

    last_e = spread_cores(whole_e, 9, 11)
    last_n.wait_recv()
    outs.append(pltpu.make_async_copy(whole_n, gn_hbm, out_sems.at[5]))
    outs[-1].start()
    last_e.wait_recv()
    outs.append(pltpu.make_async_copy(whole_e, ge_hbm, out_sems.at[6]))
    outs[-1].start()

    for copy in (swap_n, swap_e, last_n, last_e):
        copy.wait_send()
    counted(send_n, got_n, 1, 7).wait_send()
    counted(send_e, got_e, 3, 7).wait_send()
    counted(sum_yn, sum_yn, 4, 7).wait_send()
    counted(sum_ye, sum_ye, 5, 7).wait_send()
    counted(sum_xn, sum_xn, 6, 3).wait_send()
    counted(sum_xe, sum_xe, 7, 3).wait_send()
    counted(whole_n, whole_n, 8, 7).wait_send()
    counted(whole_e, whole_e, 9, 7).wait_send()
    for copy in (to_prev, to_next, give_next, give_prev):
        copy.wait_send()
    others = pl.ds(0, NDOM - 1)
    for src, dst, send, recv in (
        (out_rows, nodes, relay_send, relay_recv.at[0]),
        (back_rows, returned, ret_send, ret_recv),
    ):
        remote(src.at[others], dst.at[others], send, recv, {"dom": nxt}).wait_send()
    for copy in outs:
        copy.wait()


def finish_kernel(node_in, gx_in, ge_in, gn_in, node_out, gx_out, ge_out, gn_out, ge, gn, rows, grads_e, grads_n, sems):
    loads = [
        pltpu.make_async_copy(ge_in, ge, sems.at[0]),
        pltpu.make_async_copy(gn_in, gn, sems.at[1]),
    ]
    stores = []
    for i, (src, dst) in enumerate(((node_in, node_out), (gx_in, gx_out))):
        for j in range(2):
            here = pl.ds(j * 512, 512)
            k = 2 + 2 * i + j
            loads.append(pltpu.make_async_copy(src.at[here], rows.at[i, here], sems.at[k]))
            stores.append(pltpu.make_async_copy(rows.at[i, here], dst.at[0, here], sems.at[4 + k]))
    for copy in loads:
        copy.start()
    for load in loads[:2]:
        load.wait()
    for load, store in zip(loads[2:], stores):
        load.wait()
        store.start()
    grads_e[...] = ge[...].astype(F32).reshape(256, 256)
    stores.append(pltpu.make_async_copy(grads_e, ge_out, sems.at[10]))
    stores[-1].start()
    grads_n[...] = gn[...].astype(F32).reshape(512, 256)
    stores.append(pltpu.make_async_copy(grads_n, gn_out, sems.at[11]))
    stores[-1].start()
    for store in stores:
        store.wait()


def finish(node_out, gx, ge, gn):
    hbm = pl.BlockSpec(memory_space=pl.ANY)
    return pl.pallas_call(
        finish_kernel,
        out_shape=(
            jax.ShapeDtypeStruct((1, 1024, 256), BF),
            jax.ShapeDtypeStruct((1, 1024, 256), BF),
            jax.ShapeDtypeStruct((256, 256), F32),
            jax.ShapeDtypeStruct((512, 256), F32),
        ),
        in_specs=[hbm, hbm, hbm, hbm],
        out_specs=(hbm, hbm, hbm, hbm),
        scratch_shapes=[
            pltpu.VMEM((16, 16, 256), BF),
            pltpu.VMEM((16, 32, 256), BF),
            pltpu.VMEM((2, 1024, 256), BF),
            pltpu.VMEM((256, 256), F32),
            pltpu.VMEM((512, 256), F32),
            pltpu.SemaphoreType.DMA((12,)),
        ],
        compiler_params=pltpu.CompilerParams(vmem_limit_bytes=60 << 20),
        name="finish",
    )(node_out, gx, ge, gn)


def shards(features, send_order, adj_count, adj_target, adj_vals, w_edge, w_node, cotangent):
    vmem = pl.BlockSpec(memory_space=pltpu.VMEM)
    smem = pl.BlockSpec(memory_space=pltpu.SMEM)
    hbm = pl.BlockSpec(memory_space=pl.ANY)
    V = pltpu.VMEM
    dma = pltpu.SemaphoreType.DMA
    scale = 1.0 / math.sqrt(float(lax.axis_size("dp") * features.shape[1] * lax.axis_size("dom")))
    node_out, gx, ge, gn = pl.pallas_call(
        functools.partial(layer_kernel, scale),
        out_shape=(
            jax.ShapeDtypeStruct((1024, 256), BF),
            jax.ShapeDtypeStruct((1024, 256), BF),
            jax.ShapeDtypeStruct((16, 16, 256), BF),
            jax.ShapeDtypeStruct((16, 32, 256), BF),
        ),
        in_specs=[hbm, vmem, smem, smem, hbm, hbm, hbm, hbm],
        out_specs=(hbm, hbm, hbm, hbm),
        scratch_shapes=[
            V((1024, 256), BF),
            V((8, 4, 128, 128), BF),
            V((256, 256), BF),
            V((512, 256), BF),
            V((1024, 256), BF),
            V((64, 16, 256), BF),
            V((64, 16, 256), BF),
            V((1024, 256), F32),
            V((1024, 256), BF),
            V((1536, 1024), BF),
            V((8, 128, 512), BF),
            V((1024, 1024), BF),
            V((1024, 256), BF),
            V((1024, 256), F32),
            V((1024, 256), BF),
            V((1024, 256), F32),
            V((2, 256, 256), BF),
            V((2, 256, 256), BF),
            V((12, 128, 256), BF),
            V((1024, 256), BF),
            V((64, 16, 256), BF),
            V((64, 16, 256), BF),
            V((1024, 256), BF),
            V((1024, 256), BF),
            V((16, 32, 256), F32),
            V((16, 16, 256), F32),
            V((8, 32, 256), BF),
            V((8, 16, 256), BF),
            V((8, 32, 256), BF),
            V((8, 16, 256), BF),
            V((8, 32, 256), BF),
            V((8, 16, 256), BF),
            V((8, 32, 256), BF),
            V((8, 16, 256), BF),
            V((8, 32, 256), BF),
            V((8, 16, 256), BF),
            V((4, 32, 256), BF),
            V((4, 16, 256), BF),
            V((16, 32, 256), BF),
            V((16, 16, 256), BF),
            dma((5,)),
            dma(()),
            dma((8,)),
            dma(()),
            dma(()),
            dma((4,)),
            dma((4,)),
            dma((12,)),
            dma((12,)),
            dma((7,)),
        ],
        compiler_params=pltpu.CompilerParams(
            collective_id=0, has_side_effects=True, vmem_limit_bytes=60 << 20
        ),
        name="layer",
    )(
        features[0],
        send_order.reshape(8, 128),
        adj_count,
        adj_target.T,
        adj_vals,
        w_edge,
        w_node,
        cotangent[0],
    )
    return finish(node_out, gx, ge, gn)


def solution(mesh):
    in_specs = (
        P("dp", "dom", None),
        P("dom", None),
        P("dom"),
        P("dom", None),
        P("dom", None, None, None),
        P(),
        P(),
        P("dp", "dom", None),
    )
    out_specs = (P("dp", "dom", None), P("dp", "dom", None), P(), P())
    return jax.shard_map(shards, mesh=mesh, in_specs=in_specs, out_specs=out_specs, check_vma=False)
```

```python
import functools
import math

import jax
import jax.numpy as jnp
from jax import lax
from jax.experimental import pallas as pl
from jax.experimental.pallas import tpu as pltpu
from jax.sharding import PartitionSpec as P

NDOM = 64
BF = jnp.bfloat16
F32 = jnp.float32
NT = (((1,), (1,)), ((), ()))
TN = (((0,), (0,)), ((), ()))


def dot(a, b):
    return jnp.dot(a, b, preferred_element_type=F32)


def sigmoid(v):
    return jax.nn.sigmoid(v)


def rows_of(b):
    return pl.ds(pl.multiple_of(b * 128, 128), 128)


def remote(src, dst, send, recv, where):
    return pltpu.make_async_remote_copy(
        src_ref=src,
        dst_ref=dst,
        send_sem=send,
        recv_sem=recv,
        device_id=where,
        device_id_type=pl.DeviceIdType.MESH,
    )


def layer_kernel(
    scale,
    feat_hbm,
    order,
    cnt,
    tgt,
    vals_hbm,
    we_hbm,
    wn_hbm,
    cot_hbm,
    node_hbm,
    gx_hbm,
    ge_hbm,
    gn_hbm,
    feat,
    vals,
    we,
    wn,
    cot,
    out_rows,
    nodes,
    pre_edge,
    message,
    adj,
    adj_t,
    perm_t,
    agg,
    pre_node,
    d_node,
    d_nodes1,
    rim_out,
    rim_in,
    dwin,
    d_edge,
    back_rows,
    returned,
    node_out,
    gx_out,
    part_n,
    part_e,
    give_n,
    half_n,
    send_n,
    got_n,
    got_e,
    sum_yn,
    sum_ye,
    send_zn,
    got_zn,
    all_zn,
    sum_xe,
    whole_n,
    whole_e,
    in_sems,
    relay_send,
    relay_recv,
    ret_send,
    ret_recv,
    halo_send,
    halo_recv,
    grad_send,
    grad_recv,
    out_sems,
):
    me = lax.axis_index("dom")
    plane = lax.axis_index("dp")
    core = lax.rem(me, 2)
    row = me // 8
    col = lax.rem(me // 2, 4)
    sibling = {"dom": me + 1 - 2 * core}
    prev = lax.rem(me + NDOM - 1, NDOM)
    nxt = lax.rem(me + 1, NDOM)

    barrier = pltpu.get_barrier_semaphore()

    @pl.loop(1, NDOM)
    def _(s):
        pl.semaphore_signal(
            barrier,
            inc=1,
            device_id={"dom": lax.rem(me + s, NDOM)},
            device_id_type=pl.DeviceIdType.MESH,
        )

    for step in range(1, 8):
        for other in range(2):
            pl.semaphore_signal(
                barrier,
                inc=1,
                device_id={"dp": lax.rem(plane + step, 8), "dom": me - core + other},
                device_id_type=pl.DeviceIdType.MESH,
            )

    loads = [
        pltpu.make_async_copy(src, dst, in_sems.at[i])
        for i, (src, dst) in enumerate(
            [(feat_hbm, feat), (vals_hbm, vals), (we_hbm, we), (wn_hbm, wn), (cot_hbm, cot)]
        )
    ]
    for copy in loads:
        copy.start()

    def send_group(src, dst, send, recv, b, shift):
        for jj in range(8):
            k = b * 8 + jj
            if shift:
                remote(src.at[k], dst.at[me], send, recv, {"dom": k}).start()
                continue

            @pl.when(k != me)
            def _():
                remote(src.at[k], dst.at[me], send, recv, {"dom": k}).start()

            @pl.when(k == me)
            def _():
                pltpu.make_async_copy(src.at[k], dst.at[me], recv).start()

    loads[0].wait()
    far_first = [4, 3, 5, 2, 6, 1, 7, 0]

    lanes = lax.broadcasted_iota(jnp.int32, (128, 1024), 1)
    for r, shift in enumerate(far_first):
        b = lax.rem(row + shift, 8)
        own = jnp.broadcast_to(order[pl.ds(b, 1), :], (128, 128)).T
        hot = jnp.where(jnp.concatenate([own] * 8, axis=1) == lanes, 1.0, 0.0)
        picked = dot(hot.astype(BF), feat[...]).astype(BF)
        out_rows[pl.ds(pl.multiple_of(b * 8, 8), 8)] = picked.reshape(8, 16, 256)
        if r == 0:
            pl.semaphore_wait(barrier, NDOM - 1 + 14)
        send_group(out_rows, nodes, relay_send, relay_recv.at[row], b, shift)

    down = lax.broadcasted_iota(jnp.int32, (1024, 128), 0)
    for ib in range(8):
        mine = jnp.broadcast_to(order[ib : ib + 1, :], (1024, 128))
        perm_t[:, ib * 128 : (ib + 1) * 128] = jnp.where(mine == down, 1.0, 0.0).astype(BF)
    for copy in loads[1:]:
        copy.wait()

    @pl.loop(0, 8)
    def _(c):
        blocks = []
        for s in range(4):
            live = (cnt[c] > s).astype(jnp.int32).astype(F32)
            block = vals[c, s].astype(F32) * live
            blocks.append(block)
            adj_t[c, :, s * 128 : (s + 1) * 128] = block.T.astype(BF)
        for w in range(12):
            total = None
            for s in range(4):
                hit = (tgt[s, c] == w + 6).astype(jnp.int32).astype(F32)
                term = blocks[s] * hit
                total = term if total is None else total + term
            adj[w * 128 : (w + 1) * 128, rows_of(c)] = total.astype(BF)

    for shift in reversed(far_first):
        b = lax.rem(row + shift, 8)
        group = nodes.at[pl.ds(pl.multiple_of(b * 8, 8), 8)]
        pltpu.make_async_copy(group, group, relay_recv.at[b]).wait()
        rows = group[...].reshape(128, 256)
        v = dot(rows, we[...])
        pre_edge[rows_of(b), :] = v
        message[rows_of(b), :] = (v * sigmoid(v)).astype(BF)

    rim_out[0] = dot(adj[0:256, :], message[...]).astype(BF)
    to_prev = remote(rim_out.at[0], rim_in.at[0], halo_send.at[0], halo_recv.at[0], {"dom": prev})
    to_prev.start()
    rim_out[1] = dot(adj[1280:1536, :], message[...]).astype(BF)
    to_next = remote(rim_out.at[1], rim_in.at[1], halo_send.at[1], halo_recv.at[1], {"dom": nxt})
    to_next.start()

    def flat_nodes(lo, n):
        return nodes[lo // 16 : (lo + n) // 16].reshape(n, 256)

    def node_step(lo, n):
        here = slice(lo, lo + n)
        own = flat_nodes(lo, n)
        v = pre_node[here, :] + dot(agg[here, :], wn[256:512, :])
        sig = sigmoid(v)
        node_out[here, :] = (own.astype(F32) + v * sig).astype(BF)
        g = cot[here, :].astype(F32)
        d = (g * (sig * (1.0 + v * (1.0 - sig)))).astype(BF)
        d_node[here, :] = d
        back = lax.dot_general(d, wn[...], NT, preferred_element_type=F32)
        d_nodes1[here, :] = g + back[:, :256]
        dwin[2 + lo // 128 : 2 + (lo + n) // 128] = back[:, 256:].astype(BF).reshape(n // 128, 128, 256)

    for lo in range(0, 1024, 256):
        pre_node[lo : lo + 256, :] = dot(flat_nodes(lo, 256), wn[0:256, :])
    for lo in (256, 512, 0, 768):
        agg[lo : lo + 256, :] = dot(adj[lo + 256 : lo + 512, :], message[...]).astype(BF)
    node_step(256, 512)

    to_prev.wait_recv()
    agg[768:1024, :] = (agg[768:1024, :].astype(F32) + rim_in[0].astype(F32)).astype(BF)
    node_step(768, 256)
    give_next = remote(dwin.at[8:10], dwin.at[0:2], halo_send.at[2], halo_recv.at[2], {"dom": nxt})
    give_next.start()
    to_next.wait_recv()
    agg[0:256, :] = (agg[0:256, :].astype(F32) + rim_in[1].astype(F32)).astype(BF)
    node_step(0, 256)
    give_prev = remote(dwin.at[2:4], dwin.at[10:12], halo_send.at[3], halo_recv.at[3], {"dom": prev})
    give_prev.start()

    outs = [pltpu.make_async_copy(node_out, node_hbm, out_sems.at[0])]
    outs[0].start()

    def counted(src, dst, i, n):
        many = pl.ds(0, n)
        return remote(src.at[many], dst.at[many], grad_send.at[i], grad_recv.at[i], sibling)

    def swap_halves(total, part, give, half, i):
        part[...] = total.reshape(2, 4, 8, 8, 256)
        give[...] = part[1 - core].astype(BF)
        copy = remote(give, half, grad_send.at[i], grad_recv.at[i], sibling)
        copy.start()
        return copy

    def to_cols(src, dst, i):
        for step in (2, 1, 3):
            x = lax.rem(col + step, 4)
            k = row * 8 + x * 2 + core
            remote(src(x), dst.at[col], grad_send.at[i], grad_recv.at[i], {"dom": k}).start()

    def to_planes(src, dst, i):
        for step in (4, 3, 5, 2, 6, 1, 7):
            z = lax.rem(plane + step, 8)
            remote(src(z), dst.at[plane], grad_send.at[i], grad_recv.at[i], {"dp": z}).start()

    part = core * 8 + plane

    def to_group(src, dst, i):
        for step in (4, 3, 5, 2, 6, 1, 7, 0):
            for c in (core, 1 - core):
                if step == 0 and c is core:
                    continue
                z = lax.rem(plane + step, 8)
                where = {"dp": z, "dom": me - core + c} if step else sibling
                remote(src(c * 8 + z), dst.at[part], grad_send.at[i], grad_recv.at[i], where).start()

    def added(ref):
        total = ref[0].astype(F32)
        for i in range(1, ref.shape[0]):
            total = total + ref[i].astype(F32)
        return total

    def over_y(send, got, n, ring, i, j):
        counted(send, got, i, n).wait_recv()
        ring[row] = added(got).astype(BF)
        mine = ring.at[row]
        for step in range(1, 8):
            k = lax.rem(row + step, 8) * 8 + lax.rem(me, 8)
            remote(mine, mine, grad_send.at[j], grad_recv.at[j], {"dom": k}).start()

    def over_x(ring_y, ring, i, j):
        counted(ring_y, ring_y, i, 7).wait_recv()
        ring[col] = added(ring_y).astype(BF)
        mine = ring.at[col]
        for step in range(1, 4):
            k = row * 8 + lax.rem(col + step, 4) * 2 + core
            remote(mine, mine, grad_send.at[j], grad_recv.at[j], {"dom": k}).start()

    top = lax.dot_general(flat_nodes(0, 1024), d_node[...], TN, preferred_element_type=F32)
    low = lax.dot_general(agg[...], d_node[...], TN, preferred_element_type=F32)
    swap_n = swap_halves(jnp.concatenate([top, low], axis=0), part_n, give_n, half_n, 0)
    for lo in range(0, 1024, 256):
        v = pre_edge[lo : lo + 256, :]
        sig = sigmoid(v)
        pre_edge[lo : lo + 256, :] = sig * (1.0 + v * (1.0 - sig))

    swap_n.wait_recv()
    send_n[...] = (part_n[core] + half_n[...].astype(F32)).astype(BF)
    got_n[col] = send_n[col]
    to_cols(lambda x: send_n.at[x], got_n, 1)

    give_next.wait_recv()
    give_prev.wait_recv()
    for c in range(8):
        here = slice(c * 128, (c + 1) * 128)
        gathered = jnp.concatenate([dwin[jnp.clip(tgt[s, c] - 6, 0, 11)] for s in range(4)], axis=0)
        dm = dot(adj_t[c], gathered).astype(BF)
        d_edge[here, :] = (dm.astype(F32) * pre_edge[here, :]).astype(BF)

    edge = lax.dot_general(flat_nodes(0, 1024), d_edge[...], TN, preferred_element_type=F32)
    part_e[...] = edge.astype(BF).reshape(16, 16, 256)
    got_e[part] = part_e[part]
    to_group(lambda m: part_e.at[m], got_e, 3)

    def send_back(shifts):
        for shift in shifts:
            c = lax.rem(row + shift, 8)
            de = d_edge[rows_of(c), :]
            dn = d_nodes1[rows_of(c), :] + lax.dot_general(de, we[...], NT, preferred_element_type=F32)
            back_rows[pl.ds(pl.multiple_of(c * 8, 8), 8)] = dn.astype(BF).reshape(8, 16, 256)
            send_group(back_rows, returned, ret_send, ret_recv, c, shift)

    send_back([4])
    counted(send_n, got_n, 1, 3).wait_recv()
    send_zn[...] = added(got_n).astype(BF)
    got_zn[plane] = send_zn[plane]
    to_planes(lambda z: send_zn.at[z], got_zn, 6)
    send_back([5])
    over_y(send_zn, got_zn, 7, sum_yn, 6, 4)
    over_y(part_e, got_e, 15, sum_ye, 3, 5)
    send_back([3, 6])
    counted(sum_yn, sum_yn, 4, 7).wait_recv()
    all_zn[plane] = (added(sum_yn) * scale).astype(BF)
    to_planes(lambda z: all_zn.at[plane], all_zn, 8)
    over_x(sum_ye, sum_xe, 5, 7)
    send_back([2, 7, 1, 0])
    counted(all_zn, all_zn, 8, 7).wait_recv()
    mine_n = whole_n.at[core]
    mine_n[col] = all_zn[...]
    to_cols(lambda x: all_zn, mine_n, 11)
    counted(sum_xe, sum_xe, 7, 3).wait_recv()
    whole_e[part] = (added(sum_xe) * scale).astype(BF)
    to_group(lambda m: whole_e.at[part], whole_e, 9)
    counted(mine_n, mine_n, 11, 3).wait_recv()
    last_n = remote(mine_n, mine_n, grad_send.at[10], grad_recv.at[10], sibling)
    last_n.start()

    pltpu.make_async_copy(returned, returned, ret_recv).wait()
    rows = returned[...].reshape(1024, 256)
    for i, lo in enumerate(range(0, 1024, 256)):
        gx_out[lo : lo + 256, :] = dot(perm_t[lo : lo + 256, :], rows).astype(BF)
        here = pl.ds(lo, 256)
        outs.append(pltpu.make_async_copy(gx_out.at[here], gx_hbm.at[here], out_sems.at[1 + i]))
        outs[-1].start()

    last_n.wait_recv()
    outs.append(pltpu.make_async_copy(whole_n, gn_hbm, out_sems.at[5]))
    outs[-1].start()
    counted(whole_e, whole_e, 9, 15).wait_recv()
    outs.append(pltpu.make_async_copy(whole_e, ge_hbm, out_sems.at[6]))
    outs[-1].start()

    for copy in (swap_n, last_n):
        copy.wait_send()
    counted(send_n, got_n, 1, 3).wait_send()
    counted(send_zn, got_zn, 6, 7).wait_send()
    counted(all_zn, all_zn, 8, 7).wait_send()
    counted(mine_n, mine_n, 11, 3).wait_send()
    counted(part_e, got_e, 3, 15).wait_send()
    counted(sum_yn, sum_yn, 4, 7).wait_send()
    counted(sum_ye, sum_ye, 5, 7).wait_send()
    counted(sum_xe, sum_xe, 7, 3).wait_send()
    counted(whole_e, whole_e, 9, 15).wait_send()
    for copy in (to_prev, to_next, give_next, give_prev):
        copy.wait_send()
    others = pl.ds(0, NDOM - 1)
    for src, dst, send, recv in (
        (out_rows, nodes, relay_send, relay_recv.at[0]),
        (back_rows, returned, ret_send, ret_recv),
    ):
        remote(src.at[others], dst.at[others], send, recv, {"dom": nxt}).wait_send()
    for copy in outs:
        copy.wait()


def finish_kernel(node_in, gx_in, ge_in, gn_in, node_out, gx_out, ge_out, gn_out, ge, gn, rows, grads_e, grads_n, sems):
    loads = [
        pltpu.make_async_copy(ge_in, ge, sems.at[0]),
        pltpu.make_async_copy(gn_in, gn, sems.at[1]),
    ]
    stores = []
    for i, (src, dst) in enumerate(((node_in, node_out), (gx_in, gx_out))):
        for j in range(2):
            here = pl.ds(j * 512, 512)
            k = 2 + 2 * i + j
            loads.append(pltpu.make_async_copy(src.at[here], rows.at[i, here], sems.at[k]))
            stores.append(pltpu.make_async_copy(rows.at[i, here], dst.at[0, here], sems.at[4 + k]))
    for copy in loads:
        copy.start()
    for load in loads[:2]:
        load.wait()
    for load, store in zip(loads[2:], stores):
        load.wait()
        store.start()
    grads_e[...] = ge[...].astype(F32).reshape(256, 256)
    stores.append(pltpu.make_async_copy(grads_e, ge_out, sems.at[10]))
    stores[-1].start()
    grads_n[...] = gn[...].astype(F32).reshape(512, 256)
    stores.append(pltpu.make_async_copy(grads_n, gn_out, sems.at[11]))
    stores[-1].start()
    for store in stores:
        store.wait()


def finish(node_out, gx, ge, gn):
    hbm = pl.BlockSpec(memory_space=pl.ANY)
    return pl.pallas_call(
        finish_kernel,
        out_shape=(
            jax.ShapeDtypeStruct((1, 1024, 256), BF),
            jax.ShapeDtypeStruct((1, 1024, 256), BF),
            jax.ShapeDtypeStruct((256, 256), F32),
            jax.ShapeDtypeStruct((512, 256), F32),
        ),
        in_specs=[hbm, hbm, hbm, hbm],
        out_specs=(hbm, hbm, hbm, hbm),
        scratch_shapes=[
            pltpu.VMEM((16, 16, 256), BF),
            pltpu.VMEM((2, 4, 8, 8, 256), BF),
            pltpu.VMEM((2, 1024, 256), BF),
            pltpu.VMEM((256, 256), F32),
            pltpu.VMEM((512, 256), F32),
            pltpu.SemaphoreType.DMA((12,)),
        ],
        compiler_params=pltpu.CompilerParams(vmem_limit_bytes=60 << 20),
        name="finish",
    )(node_out, gx, ge, gn)


def shards(features, send_order, adj_count, adj_target, adj_vals, w_edge, w_node, cotangent):
    vmem = pl.BlockSpec(memory_space=pltpu.VMEM)
    smem = pl.BlockSpec(memory_space=pltpu.SMEM)
    hbm = pl.BlockSpec(memory_space=pl.ANY)
    V = pltpu.VMEM
    dma = pltpu.SemaphoreType.DMA
    scale = 1.0 / math.sqrt(float(lax.axis_size("dp") * features.shape[1] * lax.axis_size("dom")))
    node_out, gx, ge, gn = pl.pallas_call(
        functools.partial(layer_kernel, scale),
        out_shape=(
            jax.ShapeDtypeStruct((1024, 256), BF),
            jax.ShapeDtypeStruct((1024, 256), BF),
            jax.ShapeDtypeStruct((16, 16, 256), BF),
            jax.ShapeDtypeStruct((2, 4, 8, 8, 256), BF),
        ),
        in_specs=[hbm, vmem, smem, smem, hbm, hbm, hbm, hbm],
        out_specs=(hbm, hbm, hbm, hbm),
        scratch_shapes=[
            V((1024, 256), BF),
            V((8, 4, 128, 128), BF),
            V((256, 256), BF),
            V((512, 256), BF),
            V((1024, 256), BF),
            V((64, 16, 256), BF),
            V((64, 16, 256), BF),
            V((1024, 256), F32),
            V((1024, 256), BF),
            V((1536, 1024), BF),
            V((8, 128, 512), BF),
            V((1024, 1024), BF),
            V((1024, 256), BF),
            V((1024, 256), F32),
            V((1024, 256), BF),
            V((1024, 256), F32),
            V((2, 256, 256), BF),
            V((2, 256, 256), BF),
            V((12, 128, 256), BF),
            V((1024, 256), BF),
            V((64, 16, 256), BF),
            V((64, 16, 256), BF),
            V((1024, 256), BF),
            V((1024, 256), BF),
            V((2, 4, 8, 8, 256), F32),
            V((16, 16, 256), BF),
            V((4, 8, 8, 256), BF),
            V((4, 8, 8, 256), BF),
            V((4, 8, 8, 256), BF),
            V((4, 8, 8, 256), BF),
            V((16, 16, 256), BF),
            V((8, 8, 256), BF),
            V((8, 16, 256), BF),
            V((8, 8, 256), BF),
            V((8, 8, 256), BF),
            V((8, 8, 256), BF),
            V((4, 16, 256), BF),
            V((2, 4, 8, 8, 256), BF),
            V((16, 16, 256), BF),
            dma((5,)),
            dma(()),
            dma((8,)),
            dma(()),
            dma(()),
            dma((4,)),
            dma((4,)),
            dma((12,)),
            dma((12,)),
            dma((7,)),
        ],
        compiler_params=pltpu.CompilerParams(
            collective_id=0, has_side_effects=True, vmem_limit_bytes=60 << 20
        ),
        name="layer",
    )(
        features[0],
        send_order.reshape(8, 128),
        adj_count,
        adj_target.T,
        adj_vals,
        w_edge,
        w_node,
        cotangent[0],
    )
    return finish(node_out, gx, ge, gn)


def solution(mesh):
    in_specs = (
        P("dp", "dom", None),
        P("dom", None),
        P("dom"),
        P("dom", None),
        P("dom", None, None, None),
        P(),
        P(),
        P("dp", "dom", None),
    )
    out_specs = (P("dp", "dom", None), P("dp", "dom", None), P(), P())
    return jax.shard_map(shards, mesh=mesh, in_specs=in_specs, out_specs=out_specs, check_vma=False)
```

```python
import functools
import math

import jax
import jax.numpy as jnp
from jax import lax
from jax.experimental import pallas as pl
from jax.experimental.pallas import tpu as pltpu
from jax.sharding import PartitionSpec as P

NDOM = 64
BF = jnp.bfloat16
F32 = jnp.float32
NT = (((1,), (1,)), ((), ()))
TN = (((0,), (0,)), ((), ()))


def dot(a, b):
    return jnp.dot(a, b, preferred_element_type=F32)


def sigmoid(v):
    return jax.nn.sigmoid(v)


def rows_of(b):
    return pl.ds(pl.multiple_of(b * 128, 128), 128)


def remote(src, dst, send, recv, where):
    return pltpu.make_async_remote_copy(
        src_ref=src,
        dst_ref=dst,
        send_sem=send,
        recv_sem=recv,
        device_id=where,
        device_id_type=pl.DeviceIdType.MESH,
    )


def layer_kernel(
    scale,
    feat_hbm,
    order,
    cnt,
    tgt,
    vals_hbm,
    we_hbm,
    wn_hbm,
    cot_hbm,
    node_hbm,
    gx_hbm,
    ge_hbm,
    gn_hbm,
    feat,
    vals,
    we,
    wn,
    cot,
    out_rows,
    nodes,
    pre_edge,
    message,
    adj,
    adj_t,
    perm_t,
    agg,
    pre_node,
    d_node,
    d_nodes1,
    rim_out,
    rim_in,
    dwin,
    d_edge,
    back_rows,
    returned,
    node_out,
    gx_out,
    part_n,
    part_e,
    give_n,
    half_n,
    send_n,
    got_n,
    got_e,
    sum_yn,
    sum_ye,
    send_zn,
    got_zn,
    all_zn,
    sum_xe,
    whole_n,
    whole_e,
    in_sems,
    relay_send,
    relay_recv,
    ret_send,
    ret_recv,
    halo_send,
    halo_recv,
    grad_send,
    grad_recv,
    out_sems,
):
    me = lax.axis_index("dom")
    plane = lax.axis_index("dp")
    core = lax.rem(me, 2)
    row = me // 8
    col = lax.rem(me // 2, 4)
    sibling = {"dom": me + 1 - 2 * core}
    prev = lax.rem(me + NDOM - 1, NDOM)
    nxt = lax.rem(me + 1, NDOM)

    loads = [
        pltpu.make_async_copy(src, dst, in_sems.at[i])
        for i, (src, dst) in enumerate(
            [(feat_hbm, feat), (vals_hbm, vals), (we_hbm, we), (wn_hbm, wn), (cot_hbm, cot)]
        )
    ]
    for copy in loads:
        copy.start()

    barrier = pltpu.get_barrier_semaphore()

    for s in range(1, NDOM):
        pl.semaphore_signal(
            barrier,
            inc=1,
            device_id={"dom": lax.rem(me + s, NDOM)},
            device_id_type=pl.DeviceIdType.MESH,
        )

    for step in range(1, 8):
        for other in range(2):
            pl.semaphore_signal(
                barrier,
                inc=1,
                device_id={"dp": lax.rem(plane + step, 8), "dom": me - core + other},
                device_id_type=pl.DeviceIdType.MESH,
            )

    def send_group(src, dst, send, recv, b, shift):
        for jj in range(8):
            k = b * 8 + jj
            if shift:
                remote(src.at[k], dst.at[me], send, recv, {"dom": k}).start()
                continue

            @pl.when(k != me)
            def _():
                remote(src.at[k], dst.at[me], send, recv, {"dom": k}).start()

            @pl.when(k == me)
            def _():
                pltpu.make_async_copy(src.at[k], dst.at[me], recv).start()

    loads[0].wait()
    far_first = [4, 3, 5, 2, 6, 1, 7, 0]

    lanes = lax.broadcasted_iota(jnp.int32, (128, 1024), 1)
    for r, shift in enumerate(far_first):
        b = lax.rem(row + shift, 8)
        own = jnp.broadcast_to(order[pl.ds(b, 1), :], (128, 128)).T
        hot = jnp.where(jnp.concatenate([own] * 8, axis=1) == lanes, 1.0, 0.0)
        picked = dot(hot.astype(BF), feat[...]).astype(BF)
        out_rows[pl.ds(pl.multiple_of(b * 8, 8), 8)] = picked.reshape(8, 16, 256)
        if r == 0:
            pl.semaphore_wait(barrier, NDOM - 1 + 14)
        send_group(out_rows, nodes, relay_send, relay_recv.at[row], b, shift)

    down = lax.broadcasted_iota(jnp.int32, (1024, 128), 0)
    for ib in range(8):
        mine = jnp.broadcast_to(order[ib : ib + 1, :], (1024, 128))
        perm_t[:, ib * 128 : (ib + 1) * 128] = jnp.where(mine == down, 1.0, 0.0).astype(BF)
    for copy in loads[1:]:
        copy.wait()

    @pl.loop(0, 8)
    def _(c):
        blocks = []
        for s in range(4):
            live = (cnt[c] > s).astype(jnp.int32).astype(F32)
            block = vals[c, s].astype(F32) * live
            blocks.append(block)
            adj_t[c, :, s * 128 : (s + 1) * 128] = block.T.astype(BF)
        for w in range(12):
            total = None
            for s in range(4):
                hit = (tgt[s, c] == w + 6).astype(jnp.int32).astype(F32)
                term = blocks[s] * hit
                total = term if total is None else total + term
            adj[w * 128 : (w + 1) * 128, rows_of(c)] = total.astype(BF)

    for shift in reversed(far_first):
        b = lax.rem(row + shift, 8)
        group = nodes.at[pl.ds(pl.multiple_of(b * 8, 8), 8)]
        pltpu.make_async_copy(group, group, relay_recv.at[b]).wait()
        rows = group[...].reshape(128, 256)
        v = dot(rows, we[...])
        pre_edge[rows_of(b), :] = v
        message[rows_of(b), :] = (v * sigmoid(v)).astype(BF)

    rim_out[0] = dot(adj[0:256, :], message[...]).astype(BF)
    to_prev = remote(rim_out.at[0], rim_in.at[0], halo_send.at[0], halo_recv.at[0], {"dom": prev})
    to_prev.start()
    rim_out[1] = dot(adj[1280:1536, :], message[...]).astype(BF)
    to_next = remote(rim_out.at[1], rim_in.at[1], halo_send.at[1], halo_recv.at[1], {"dom": nxt})
    to_next.start()

    def flat_nodes(lo, n):
        return nodes[lo // 16 : (lo + n) // 16].reshape(n, 256)

    def node_step(lo, n):
        here = slice(lo, lo + n)
        own = flat_nodes(lo, n)
        v = pre_node[here, :] + dot(agg[here, :], wn[256:512, :])
        sig = sigmoid(v)
        node_out[here, :] = (own.astype(F32) + v * sig).astype(BF)
        g = cot[here, :].astype(F32)
        d = (g * (sig * (1.0 + v * (1.0 - sig)))).astype(BF)
        d_node[here, :] = d
        back = lax.dot_general(d, wn[...], NT, preferred_element_type=F32)
        d_nodes1[here, :] = g + back[:, :256]
        dwin[2 + lo // 128 : 2 + (lo + n) // 128] = back[:, 256:].astype(BF).reshape(n // 128, 128, 256)

    for lo in range(0, 1024, 256):
        pre_node[lo : lo + 256, :] = dot(flat_nodes(lo, 256), wn[0:256, :])
    for lo in (256, 512, 0, 768):
        agg[lo : lo + 256, :] = dot(adj[lo + 256 : lo + 512, :], message[...]).astype(BF)
    node_step(256, 512)

    to_prev.wait_recv()
    agg[768:1024, :] = (agg[768:1024, :].astype(F32) + rim_in[0].astype(F32)).astype(BF)
    node_step(768, 256)
    give_next = remote(dwin.at[8:10], dwin.at[0:2], halo_send.at[2], halo_recv.at[2], {"dom": nxt})
    give_next.start()
    to_next.wait_recv()
    agg[0:256, :] = (agg[0:256, :].astype(F32) + rim_in[1].astype(F32)).astype(BF)
    node_step(0, 256)
    give_prev = remote(dwin.at[2:4], dwin.at[10:12], halo_send.at[3], halo_recv.at[3], {"dom": prev})
    give_prev.start()

    outs = [pltpu.make_async_copy(node_out, node_hbm, out_sems.at[0])]
    outs[0].start()

    def counted(src, dst, i, n):
        many = pl.ds(0, n)
        return remote(src.at[many], dst.at[many], grad_send.at[i], grad_recv.at[i], sibling)

    def swap_halves(total, part, give, half, i):
        part[...] = total.reshape(2, 4, 8, 8, 256)
        give[...] = part[1 - core].astype(BF)
        copy = remote(give, half, grad_send.at[i], grad_recv.at[i], sibling)
        copy.start()
        return copy

    def to_cols(src, dst, i):
        for step in (2, 1, 3):
            x = lax.rem(col + step, 4)
            k = row * 8 + x * 2 + core
            remote(src(x), dst.at[col], grad_send.at[i], grad_recv.at[i], {"dom": k}).start()

    def to_planes(src, dst, i):
        for step in (4, 3, 5, 2, 6, 1, 7):
            z = lax.rem(plane + step, 8)
            remote(src(z), dst.at[plane], grad_send.at[i], grad_recv.at[i], {"dp": z}).start()

    part = core * 8 + plane

    def to_group(src, dst, i):
        for step in (4, 3, 5, 2, 6, 1, 7, 0):
            for c in (core, 1 - core):
                if step == 0 and c is core:
                    continue
                z = lax.rem(plane + step, 8)
                where = {"dp": z, "dom": me - core + c} if step else sibling
                remote(src(c * 8 + z), dst.at[part], grad_send.at[i], grad_recv.at[i], where).start()

    def added(ref):
        total = ref[0].astype(F32)
        for i in range(1, ref.shape[0]):
            total = total + ref[i].astype(F32)
        return total

    def over_y(send, got, n, ring, i, j):
        counted(send, got, i, n).wait_recv()
        ring[row] = added(got).astype(BF)
        mine = ring.at[row]
        for step in range(1, 8):
            k = lax.rem(row + step, 8) * 8 + lax.rem(me, 8)
            remote(mine, mine, grad_send.at[j], grad_recv.at[j], {"dom": k}).start()

    def over_x(ring_y, ring, i, j):
        counted(ring_y, ring_y, i, 7).wait_recv()
        ring[col] = added(ring_y).astype(BF)
        mine = ring.at[col]
        for step in range(1, 4):
            k = row * 8 + lax.rem(col + step, 4) * 2 + core
            remote(mine, mine, grad_send.at[j], grad_recv.at[j], {"dom": k}).start()

    top = lax.dot_general(flat_nodes(0, 1024), d_node[...], TN, preferred_element_type=F32)
    low = lax.dot_general(agg[...], d_node[...], TN, preferred_element_type=F32)
    swap_n = swap_halves(jnp.concatenate([top, low], axis=0), part_n, give_n, half_n, 0)
    for lo in range(0, 1024, 256):
        v = pre_edge[lo : lo + 256, :]
        sig = sigmoid(v)
        pre_edge[lo : lo + 256, :] = sig * (1.0 + v * (1.0 - sig))

    swap_n.wait_recv()
    send_n[...] = (part_n[core] + half_n[...].astype(F32)).astype(BF)
    got_n[col] = send_n[col]
    to_cols(lambda x: send_n.at[x], got_n, 1)

    give_next.wait_recv()
    give_prev.wait_recv()
    for c in range(8):
        here = slice(c * 128, (c + 1) * 128)
        gathered = jnp.concatenate([dwin[jnp.clip(tgt[s, c] - 6, 0, 11)] for s in range(4)], axis=0)
        dm = dot(adj_t[c], gathered).astype(BF)
        d_edge[here, :] = (dm.astype(F32) * pre_edge[here, :]).astype(BF)

    edge = lax.dot_general(flat_nodes(0, 1024), d_edge[...], TN, preferred_element_type=F32)
    part_e[...] = edge.astype(BF).reshape(16, 16, 256)
    got_e[part] = part_e[part]
    to_group(lambda m: part_e.at[m], got_e, 3)

    def send_back(shifts):
        for shift in shifts:
            c = lax.rem(row + shift, 8)
            de = d_edge[rows_of(c), :]
            dn = d_nodes1[rows_of(c), :] + lax.dot_general(de, we[...], NT, preferred_element_type=F32)
            back_rows[pl.ds(pl.multiple_of(c * 8, 8), 8)] = dn.astype(BF).reshape(8, 16, 256)
            send_group(back_rows, returned, ret_send, ret_recv, c, shift)

    send_back([4])
    counted(send_n, got_n, 1, 3).wait_recv()
    send_zn[...] = added(got_n).astype(BF)
    got_zn[plane] = send_zn[plane]
    to_planes(lambda z: send_zn.at[z], got_zn, 6)
    send_back([5])
    over_y(send_zn, got_zn, 7, sum_yn, 6, 4)
    counted(part_e, got_e, 3, 15).wait_recv()
    sum_xe[col] = added(got_e).astype(BF)
    to_cols(lambda x: sum_xe.at[col], sum_xe, 7)
    send_back([3, 6])
    counted(sum_yn, sum_yn, 4, 7).wait_recv()
    all_zn[plane] = (added(sum_yn) * scale).astype(BF)
    to_planes(lambda z: all_zn.at[plane], all_zn, 8)
    over_y(sum_xe, sum_xe, 3, sum_ye, 7, 5)
    send_back([2, 7, 1, 0])
    counted(all_zn, all_zn, 8, 7).wait_recv()
    mine_n = whole_n.at[core]
    mine_n[col] = all_zn[...]
    to_cols(lambda x: all_zn, mine_n, 11)
    counted(sum_ye, sum_ye, 5, 7).wait_recv()
    whole_e[part] = (added(sum_ye) * scale).astype(BF)
    to_group(lambda m: whole_e.at[part], whole_e, 9)
    counted(mine_n, mine_n, 11, 3).wait_recv()
    last_n = remote(mine_n, mine_n, grad_send.at[10], grad_recv.at[10], sibling)
    last_n.start()

    pltpu.make_async_copy(returned, returned, ret_recv).wait()
    rows = returned[...].reshape(1024, 256)
    for i, lo in enumerate(range(0, 1024, 256)):
        gx_out[lo : lo + 256, :] = dot(perm_t[lo : lo + 256, :], rows).astype(BF)
        here = pl.ds(lo, 256)
        outs.append(pltpu.make_async_copy(gx_out.at[here], gx_hbm.at[here], out_sems.at[1 + i]))
        outs[-1].start()

    last_n.wait_recv()
    outs.append(pltpu.make_async_copy(whole_n, gn_hbm, out_sems.at[5]))
    outs[-1].start()
    counted(whole_e, whole_e, 9, 15).wait_recv()
    outs.append(pltpu.make_async_copy(whole_e, ge_hbm, out_sems.at[6]))
    outs[-1].start()

    for copy in (swap_n, last_n):
        copy.wait_send()
    counted(send_n, got_n, 1, 3).wait_send()
    counted(send_zn, got_zn, 6, 7).wait_send()
    counted(all_zn, all_zn, 8, 7).wait_send()
    counted(mine_n, mine_n, 11, 3).wait_send()
    counted(part_e, got_e, 3, 15).wait_send()
    counted(sum_yn, sum_yn, 4, 7).wait_send()
    counted(sum_ye, sum_ye, 5, 7).wait_send()
    counted(sum_xe, sum_xe, 7, 3).wait_send()
    counted(whole_e, whole_e, 9, 15).wait_send()
    for copy in (to_prev, to_next, give_next, give_prev):
        copy.wait_send()
    others = pl.ds(0, NDOM - 1)
    for src, dst, send, recv in (
        (out_rows, nodes, relay_send, relay_recv.at[0]),
        (back_rows, returned, ret_send, ret_recv),
    ):
        remote(src.at[others], dst.at[others], send, recv, {"dom": nxt}).wait_send()
    for copy in outs:
        copy.wait()


def finish_kernel(node_in, gx_in, ge_in, gn_in, node_out, gx_out, ge_out, gn_out, ge, gn, rows, grads_e, grads_n, sems):
    loads = [
        pltpu.make_async_copy(ge_in, ge, sems.at[0]),
        pltpu.make_async_copy(gn_in, gn, sems.at[1]),
    ]
    stores = []
    for i, (src, dst) in enumerate(((node_in, node_out), (gx_in, gx_out))):
        for j in range(2):
            here = pl.ds(j * 512, 512)
            k = 2 + 2 * i + j
            loads.append(pltpu.make_async_copy(src.at[here], rows.at[i, here], sems.at[k]))
            stores.append(pltpu.make_async_copy(rows.at[i, here], dst.at[0, here], sems.at[4 + k]))
    for copy in loads:
        copy.start()
    for load in loads[:2]:
        load.wait()
    for load, store in zip(loads[2:], stores):
        load.wait()
        store.start()
    grads_e[...] = ge[...].astype(F32).reshape(256, 256)
    stores.append(pltpu.make_async_copy(grads_e, ge_out, sems.at[10]))
    stores[-1].start()
    grads_n[...] = gn[...].astype(F32).reshape(512, 256)
    stores.append(pltpu.make_async_copy(grads_n, gn_out, sems.at[11]))
    stores[-1].start()
    for store in stores:
        store.wait()


def finish(node_out, gx, ge, gn):
    hbm = pl.BlockSpec(memory_space=pl.ANY)
    return pl.pallas_call(
        finish_kernel,
        out_shape=(
            jax.ShapeDtypeStruct((1, 1024, 256), BF),
            jax.ShapeDtypeStruct((1, 1024, 256), BF),
            jax.ShapeDtypeStruct((256, 256), F32),
            jax.ShapeDtypeStruct((512, 256), F32),
        ),
        in_specs=[hbm, hbm, hbm, hbm],
        out_specs=(hbm, hbm, hbm, hbm),
        scratch_shapes=[
            pltpu.VMEM((16, 16, 256), BF),
            pltpu.VMEM((2, 4, 8, 8, 256), BF),
            pltpu.VMEM((2, 1024, 256), BF),
            pltpu.VMEM((256, 256), F32),
            pltpu.VMEM((512, 256), F32),
            pltpu.SemaphoreType.DMA((12,)),
        ],
        compiler_params=pltpu.CompilerParams(vmem_limit_bytes=60 << 20),
        name="finish",
    )(node_out, gx, ge, gn)


def shards(features, send_order, adj_count, adj_target, adj_vals, w_edge, w_node, cotangent):
    vmem = pl.BlockSpec(memory_space=pltpu.VMEM)
    smem = pl.BlockSpec(memory_space=pltpu.SMEM)
    hbm = pl.BlockSpec(memory_space=pl.ANY)
    V = pltpu.VMEM
    dma = pltpu.SemaphoreType.DMA
    scale = 1.0 / math.sqrt(float(lax.axis_size("dp") * features.shape[1] * lax.axis_size("dom")))
    node_out, gx, ge, gn = pl.pallas_call(
        functools.partial(layer_kernel, scale),
        out_shape=(
            jax.ShapeDtypeStruct((1024, 256), BF),
            jax.ShapeDtypeStruct((1024, 256), BF),
            jax.ShapeDtypeStruct((16, 16, 256), BF),
            jax.ShapeDtypeStruct((2, 4, 8, 8, 256), BF),
        ),
        in_specs=[hbm, vmem, smem, smem, hbm, hbm, hbm, hbm],
        out_specs=(hbm, hbm, hbm, hbm),
        scratch_shapes=[
            V((1024, 256), BF),
            V((8, 4, 128, 128), BF),
            V((256, 256), BF),
            V((512, 256), BF),
            V((1024, 256), BF),
            V((64, 16, 256), BF),
            V((64, 16, 256), BF),
            V((1024, 256), F32),
            V((1024, 256), BF),
            V((1536, 1024), BF),
            V((8, 128, 512), BF),
            V((1024, 1024), BF),
            V((1024, 256), BF),
            V((1024, 256), F32),
            V((1024, 256), BF),
            V((1024, 256), F32),
            V((2, 256, 256), BF),
            V((2, 256, 256), BF),
            V((12, 128, 256), BF),
            V((1024, 256), BF),
            V((64, 16, 256), BF),
            V((64, 16, 256), BF),
            V((1024, 256), BF),
            V((1024, 256), BF),
            V((2, 4, 8, 8, 256), F32),
            V((16, 16, 256), BF),
            V((4, 8, 8, 256), BF),
            V((4, 8, 8, 256), BF),
            V((4, 8, 8, 256), BF),
            V((4, 8, 8, 256), BF),
            V((16, 16, 256), BF),
            V((8, 8, 256), BF),
            V((8, 16, 256), BF),
            V((8, 8, 256), BF),
            V((8, 8, 256), BF),
            V((8, 8, 256), BF),
            V((4, 16, 256), BF),
            V((2, 4, 8, 8, 256), BF),
            V((16, 16, 256), BF),
            dma((5,)),
            dma(()),
            dma((8,)),
            dma(()),
            dma(()),
            dma((4,)),
            dma((4,)),
            dma((12,)),
            dma((12,)),
            dma((7,)),
        ],
        compiler_params=pltpu.CompilerParams(
            collective_id=0, has_side_effects=True, vmem_limit_bytes=60 << 20
        ),
        name="layer",
    )(
        features[0],
        send_order.reshape(8, 128),
        adj_count,
        adj_target.T,
        adj_vals,
        w_edge,
        w_node,
        cotangent[0],
    )
    return finish(node_out, gx, ge, gn)


def solution(mesh):
    in_specs = (
        P("dp", "dom", None),
        P("dom", None),
        P("dom"),
        P("dom", None),
        P("dom", None, None, None),
        P(),
        P(),
        P("dp", "dom", None),
    )
    out_specs = (P("dp", "dom", None), P("dp", "dom", None), P(), P())
    return jax.shard_map(shards, mesh=mesh, in_specs=in_specs, out_specs=out_specs, check_vma=False)
```

```python
import functools
import math

import jax
import jax.numpy as jnp
from jax import lax
from jax.experimental import pallas as pl
from jax.experimental.pallas import tpu as pltpu
from jax.sharding import PartitionSpec as P

NDOM = 64
BF = jnp.bfloat16
F32 = jnp.float32
NT = (((1,), (1,)), ((), ()))
TN = (((0,), (0,)), ((), ()))


def dot(a, b):
    return jnp.dot(a, b, preferred_element_type=F32)


def sigmoid(v):
    return jax.nn.sigmoid(v)


def rows_of(b):
    return pl.ds(pl.multiple_of(b * 128, 128), 128)


def remote(src, dst, send, recv, where):
    return pltpu.make_async_remote_copy(
        src_ref=src,
        dst_ref=dst,
        send_sem=send,
        recv_sem=recv,
        device_id=where,
        device_id_type=pl.DeviceIdType.MESH,
    )


def layer_kernel(
    scale,
    feat_hbm,
    order,
    cnt,
    tgt,
    vals_hbm,
    we_hbm,
    wn_hbm,
    cot_hbm,
    node_hbm,
    gx_hbm,
    ge_hbm,
    gn_hbm,
    feat,
    vals,
    we,
    wn,
    cot,
    out_rows,
    nodes,
    pre_edge,
    message,
    adj,
    adj_t,
    perm_t,
    agg,
    pre_node,
    d_node,
    d_nodes1,
    rim_out,
    rim_in,
    dwin,
    d_edge,
    back_rows,
    returned,
    node_out,
    gx_out,
    part_n,
    part_e,
    give_n,
    half_n,
    send_n,
    got_n,
    got_e,
    sum_yn,
    sum_ye,
    send_zn,
    got_zn,
    all_zn,
    sum_xe,
    whole_n,
    whole_e,
    in_sems,
    relay_send,
    relay_recv,
    ret_send,
    ret_recv,
    halo_send,
    halo_recv,
    grad_send,
    grad_recv,
    out_sems,
):
    me = lax.axis_index("dom")
    plane = lax.axis_index("dp")
    core = lax.rem(me, 2)
    row = me // 8
    col = lax.rem(me // 2, 4)
    sibling = {"dom": me + 1 - 2 * core}
    prev = lax.rem(me + NDOM - 1, NDOM)
    nxt = lax.rem(me + 1, NDOM)

    loads = [
        pltpu.make_async_copy(src, dst, in_sems.at[i])
        for i, (src, dst) in enumerate(
            [(feat_hbm, feat), (vals_hbm, vals), (we_hbm, we), (wn_hbm, wn), (cot_hbm, cot)]
        )
    ]
    for copy in loads:
        copy.start()

    barrier = pltpu.get_barrier_semaphore()

    for s in range(1, NDOM):
        pl.semaphore_signal(
            barrier,
            inc=1,
            device_id={"dom": lax.rem(me + s, NDOM)},
            device_id_type=pl.DeviceIdType.MESH,
        )

    for step in range(1, 8):
        for other in range(2):
            pl.semaphore_signal(
                barrier,
                inc=1,
                device_id={"dp": lax.rem(plane + step, 8), "dom": me - core + other},
                device_id_type=pl.DeviceIdType.MESH,
            )

    def send_group(src, dst, send, recv, b, shift):
        for jj in range(8):
            k = b * 8 + jj
            if shift:
                remote(src.at[k], dst.at[me], send, recv, {"dom": k}).start()
                continue

            @pl.when(k != me)
            def _():
                remote(src.at[k], dst.at[me], send, recv, {"dom": k}).start()

            @pl.when(k == me)
            def _():
                pltpu.make_async_copy(src.at[k], dst.at[me], recv).start()

    loads[0].wait()
    far_first = [4, 3, 5, 2, 6, 1, 7, 0]

    lanes = lax.broadcasted_iota(jnp.int32, (128, 1024), 1)
    for r, shift in enumerate(far_first):
        b = lax.rem(row + shift, 8)
        own = jnp.broadcast_to(order[pl.ds(b, 1), :], (128, 128)).T
        hot = jnp.where(jnp.concatenate([own] * 8, axis=1) == lanes, 1.0, 0.0)
        picked = dot(hot.astype(BF), feat[...]).astype(BF)
        out_rows[pl.ds(pl.multiple_of(b * 8, 8), 8)] = picked.reshape(8, 16, 256)
        if r == 0:
            pl.semaphore_wait(barrier, NDOM - 1 + 14)
        send_group(out_rows, nodes, relay_send, relay_recv.at[row], b, shift)

    down = lax.broadcasted_iota(jnp.int32, (1024, 128), 0)
    for ib in range(8):
        mine = jnp.broadcast_to(order[ib : ib + 1, :], (1024, 128))
        perm_t[:, ib * 128 : (ib + 1) * 128] = jnp.where(mine == down, 1.0, 0.0).astype(BF)
    for copy in loads[1:]:
        copy.wait()

    @pl.loop(0, 8)
    def _(c):
        blocks = []
        for s in range(4):
            live = (cnt[c] > s).astype(jnp.int32).astype(F32)
            block = vals[c, s].astype(F32) * live
            blocks.append(block)
            adj_t[c, :, s * 128 : (s + 1) * 128] = block.T.astype(BF)
        for w in range(12):
            total = None
            for s in range(4):
                hit = (tgt[s, c] == w + 6).astype(jnp.int32).astype(F32)
                term = blocks[s] * hit
                total = term if total is None else total + term
            adj[w * 128 : (w + 1) * 128, rows_of(c)] = total.astype(BF)

    for shift in reversed(far_first):
        b = lax.rem(row + shift, 8)
        group = nodes.at[pl.ds(pl.multiple_of(b * 8, 8), 8)]
        pltpu.make_async_copy(group, group, relay_recv.at[b]).wait()
        rows = group[...].reshape(128, 256)
        v = dot(rows, we[...])
        pre_edge[rows_of(b), :] = v
        message[rows_of(b), :] = (v * sigmoid(v)).astype(BF)

    rim_out[0] = dot(adj[0:256, :], message[...]).astype(BF)
    to_prev = remote(rim_out.at[0], rim_in.at[0], halo_send.at[0], halo_recv.at[0], {"dom": prev})
    to_prev.start()
    rim_out[1] = dot(adj[1280:1536, :], message[...]).astype(BF)
    to_next = remote(rim_out.at[1], rim_in.at[1], halo_send.at[1], halo_recv.at[1], {"dom": nxt})
    to_next.start()

    def flat_nodes(lo, n):
        return nodes[lo // 16 : (lo + n) // 16].reshape(n, 256)

    def node_step(lo, n):
        here = slice(lo, lo + n)
        own = flat_nodes(lo, n)
        v = pre_node[here, :] + dot(agg[here, :], wn[256:512, :])
        sig = sigmoid(v)
        node_out[here, :] = (own.astype(F32) + v * sig).astype(BF)
        g = cot[here, :].astype(F32)
        d = (g * (sig * (1.0 + v * (1.0 - sig)))).astype(BF)
        d_node[here, :] = d
        back = lax.dot_general(d, wn[...], NT, preferred_element_type=F32)
        d_nodes1[here, :] = g + back[:, :256]
        dwin[2 + lo // 128 : 2 + (lo + n) // 128] = back[:, 256:].astype(BF).reshape(n // 128, 128, 256)

    for lo in range(0, 1024, 256):
        pre_node[lo : lo + 256, :] = dot(flat_nodes(lo, 256), wn[0:256, :])
    for lo in (256, 512, 0, 768):
        agg[lo : lo + 256, :] = dot(adj[lo + 256 : lo + 512, :], message[...]).astype(BF)
    node_step(256, 512)

    to_prev.wait_recv()
    agg[768:1024, :] = (agg[768:1024, :].astype(F32) + rim_in[0].astype(F32)).astype(BF)
    node_step(768, 256)
    give_next = remote(dwin.at[8:10], dwin.at[0:2], halo_send.at[2], halo_recv.at[2], {"dom": nxt})
    give_next.start()
    to_next.wait_recv()
    agg[0:256, :] = (agg[0:256, :].astype(F32) + rim_in[1].astype(F32)).astype(BF)
    node_step(0, 256)
    give_prev = remote(dwin.at[2:4], dwin.at[10:12], halo_send.at[3], halo_recv.at[3], {"dom": prev})
    give_prev.start()

    outs = [pltpu.make_async_copy(node_out, node_hbm, out_sems.at[0])]
    outs[0].start()

    def counted(src, dst, i, n):
        many = pl.ds(0, n)
        return remote(src.at[many], dst.at[many], grad_send.at[i], grad_recv.at[i], sibling)

    def swap_halves(total, part, give, half, i):
        part[...] = total.reshape(2, 4, 8, 8, 256)
        give[...] = part[1 - core].astype(BF)
        copy = remote(give, half, grad_send.at[i], grad_recv.at[i], sibling)
        copy.start()
        return copy

    def to_cols(src, dst, i):
        for step in (2, 1, 3):
            x = lax.rem(col + step, 4)
            k = row * 8 + x * 2 + core
            remote(src(x), dst.at[col], grad_send.at[i], grad_recv.at[i], {"dom": k}).start()

    def to_planes(src, dst, i):
        for step in (4, 3, 5, 2, 6, 1, 7):
            z = lax.rem(plane + step, 8)
            remote(src(z), dst.at[plane], grad_send.at[i], grad_recv.at[i], {"dp": z}).start()

    part = core * 8 + plane

    def to_group(src, dst, i):
        for step in (4, 3, 5, 2, 6, 1, 7, 0):
            for c in (core, 1 - core):
                if step == 0 and c is core:
                    continue
                z = lax.rem(plane + step, 8)
                where = {"dp": z, "dom": me - core + c} if step else sibling
                remote(src(c * 8 + z), dst.at[part], grad_send.at[i], grad_recv.at[i], where).start()

    def added(ref):
        total = ref[0].astype(F32)
        for i in range(1, ref.shape[0]):
            total = total + ref[i].astype(F32)
        return total

    def over_y(send, got, n, ring, i, j):
        counted(send, got, i, n).wait_recv()
        ring[row] = added(got).astype(BF)
        mine = ring.at[row]
        for step in range(1, 8):
            k = lax.rem(row + step, 8) * 8 + lax.rem(me, 8)
            remote(mine, mine, grad_send.at[j], grad_recv.at[j], {"dom": k}).start()

    def over_x(ring_y, ring, i, j):
        counted(ring_y, ring_y, i, 7).wait_recv()
        ring[col] = added(ring_y).astype(BF)
        mine = ring.at[col]
        for step in range(1, 4):
            k = row * 8 + lax.rem(col + step, 4) * 2 + core
            remote(mine, mine, grad_send.at[j], grad_recv.at[j], {"dom": k}).start()

    top = lax.dot_general(flat_nodes(0, 1024), d_node[...], TN, preferred_element_type=F32)
    low = lax.dot_general(agg[...], d_node[...], TN, preferred_element_type=F32)
    swap_n = swap_halves(jnp.concatenate([top, low], axis=0), part_n, give_n, half_n, 0)
    for lo in range(0, 1024, 256):
        v = pre_edge[lo : lo + 256, :]
        sig = sigmoid(v)
        pre_edge[lo : lo + 256, :] = sig * (1.0 + v * (1.0 - sig))

    swap_n.wait_recv()
    send_n[...] = (part_n[core] + half_n[...].astype(F32)).astype(BF)
    got_n[col] = send_n[col]
    to_cols(lambda x: send_n.at[x], got_n, 1)

    give_next.wait_recv()
    give_prev.wait_recv()
    for c in range(8):
        here = slice(c * 128, (c + 1) * 128)
        gathered = jnp.concatenate([dwin[jnp.clip(tgt[s, c] - 6, 0, 11)] for s in range(4)], axis=0)
        dm = dot(adj_t[c], gathered).astype(BF)
        d_edge[here, :] = (dm.astype(F32) * pre_edge[here, :]).astype(BF)

    edge = lax.dot_general(flat_nodes(0, 1024), d_edge[...], TN, preferred_element_type=F32)
    part_e[...] = edge.astype(BF).reshape(16, 16, 256)
    got_e[part] = part_e[part]
    to_group(lambda m: part_e.at[m], got_e, 3)

    def send_back(shifts):
        for shift in shifts:
            c = lax.rem(row + shift, 8)
            de = d_edge[rows_of(c), :]
            dn = d_nodes1[rows_of(c), :] + lax.dot_general(de, we[...], NT, preferred_element_type=F32)
            back_rows[pl.ds(pl.multiple_of(c * 8, 8), 8)] = dn.astype(BF).reshape(8, 16, 256)
            send_group(back_rows, returned, ret_send, ret_recv, c, shift)

    send_back([4])
    counted(send_n, got_n, 1, 3).wait_recv()
    send_zn[...] = added(got_n).astype(BF)
    got_zn[plane] = send_zn[plane]
    to_planes(lambda z: send_zn.at[z], got_zn, 6)
    send_back([5])
    over_y(send_zn, got_zn, 7, sum_yn, 6, 4)
    counted(part_e, got_e, 3, 15).wait_recv()
    sum_xe[col] = added(got_e).astype(BF)
    to_cols(lambda x: sum_xe.at[col], sum_xe, 7)
    send_back([3, 6])
    counted(sum_yn, sum_yn, 4, 7).wait_recv()
    all_zn[plane] = (added(sum_yn) * scale).astype(BF)
    to_planes(lambda z: all_zn.at[plane], all_zn, 8)
    over_y(sum_xe, sum_xe, 3, sum_ye, 7, 5)
    send_back([2, 7, 1, 0])
    counted(all_zn, all_zn, 8, 7).wait_recv()
    mine_n = core * 4 + col
    whole_n[mine_n] = all_zn[...]
    for step in (2, 1, 3, 0):
        for c in (core, 1 - core):
            if step == 0 and c is core:
                continue
            k = row * 8 + lax.rem(col + step, 4) * 2 + c
            remote(all_zn, whole_n.at[mine_n], grad_send.at[11], grad_recv.at[11], {"dom": k}).start()
    counted(sum_ye, sum_ye, 5, 7).wait_recv()
    whole_e[part] = (added(sum_ye) * scale).astype(BF)
    to_group(lambda m: whole_e.at[part], whole_e, 9)
    pltpu.make_async_copy(returned, returned, ret_recv).wait()
    rows = returned[...].reshape(1024, 256)
    for i, lo in enumerate(range(0, 1024, 256)):
        gx_out[lo : lo + 256, :] = dot(perm_t[lo : lo + 256, :], rows).astype(BF)
        here = pl.ds(lo, 256)
        outs.append(pltpu.make_async_copy(gx_out.at[here], gx_hbm.at[here], out_sems.at[1 + i]))
        outs[-1].start()

    counted(whole_n, whole_n, 11, 7).wait_recv()
    outs.append(pltpu.make_async_copy(whole_n, gn_hbm, out_sems.at[5]))
    outs[-1].start()
    counted(whole_e, whole_e, 9, 15).wait_recv()
    outs.append(pltpu.make_async_copy(whole_e, ge_hbm, out_sems.at[6]))
    outs[-1].start()

    swap_n.wait_send()
    counted(send_n, got_n, 1, 3).wait_send()
    counted(send_zn, got_zn, 6, 7).wait_send()
    counted(all_zn, all_zn, 8, 7).wait_send()
    counted(whole_n, whole_n, 11, 7).wait_send()
    counted(part_e, got_e, 3, 15).wait_send()
    counted(sum_yn, sum_yn, 4, 7).wait_send()
    counted(sum_ye, sum_ye, 5, 7).wait_send()
    counted(sum_xe, sum_xe, 7, 3).wait_send()
    counted(whole_e, whole_e, 9, 15).wait_send()
    for copy in (to_prev, to_next, give_next, give_prev):
        copy.wait_send()
    others = pl.ds(0, NDOM - 1)
    for src, dst, send, recv in (
        (out_rows, nodes, relay_send, relay_recv.at[0]),
        (back_rows, returned, ret_send, ret_recv),
    ):
        remote(src.at[others], dst.at[others], send, recv, {"dom": nxt}).wait_send()
    for copy in outs:
        copy.wait()


def finish_kernel(node_in, gx_in, ge_in, gn_in, node_out, gx_out, ge_out, gn_out, ge, gn, rows, grads_e, grads_n, sems):
    loads = [
        pltpu.make_async_copy(ge_in, ge, sems.at[0]),
        pltpu.make_async_copy(gn_in, gn, sems.at[1]),
    ]
    stores = []
    for i, (src, dst) in enumerate(((node_in, node_out), (gx_in, gx_out))):
        for j in range(2):
            here = pl.ds(j * 512, 512)
            k = 2 + 2 * i + j
            loads.append(pltpu.make_async_copy(src.at[here], rows.at[i, here], sems.at[k]))
            stores.append(pltpu.make_async_copy(rows.at[i, here], dst.at[0, here], sems.at[4 + k]))
    for copy in loads:
        copy.start()
    for load in loads[:2]:
        load.wait()
    for load, store in zip(loads[2:], stores):
        load.wait()
        store.start()
    grads_e[...] = ge[...].astype(F32).reshape(256, 256)
    stores.append(pltpu.make_async_copy(grads_e, ge_out, sems.at[10]))
    stores[-1].start()
    grads_n[...] = gn[...].astype(F32).reshape(512, 256)
    stores.append(pltpu.make_async_copy(grads_n, gn_out, sems.at[11]))
    stores[-1].start()
    for store in stores:
        store.wait()


def finish(node_out, gx, ge, gn):
    hbm = pl.BlockSpec(memory_space=pl.ANY)
    return pl.pallas_call(
        finish_kernel,
        out_shape=(
            jax.ShapeDtypeStruct((1, 1024, 256), BF),
            jax.ShapeDtypeStruct((1, 1024, 256), BF),
            jax.ShapeDtypeStruct((256, 256), F32),
            jax.ShapeDtypeStruct((512, 256), F32),
        ),
        in_specs=[hbm, hbm, hbm, hbm],
        out_specs=(hbm, hbm, hbm, hbm),
        scratch_shapes=[
            pltpu.VMEM((16, 16, 256), BF),
            pltpu.VMEM((8, 8, 8, 256), BF),
            pltpu.VMEM((2, 1024, 256), BF),
            pltpu.VMEM((256, 256), F32),
            pltpu.VMEM((512, 256), F32),
            pltpu.SemaphoreType.DMA((12,)),
        ],
        compiler_params=pltpu.CompilerParams(vmem_limit_bytes=60 << 20),
        name="finish",
    )(node_out, gx, ge, gn)


def shards(features, send_order, adj_count, adj_target, adj_vals, w_edge, w_node, cotangent):
    vmem = pl.BlockSpec(memory_space=pltpu.VMEM)
    smem = pl.BlockSpec(memory_space=pltpu.SMEM)
    hbm = pl.BlockSpec(memory_space=pl.ANY)
    V = pltpu.VMEM
    dma = pltpu.SemaphoreType.DMA
    scale = 1.0 / math.sqrt(float(lax.axis_size("dp") * features.shape[1] * lax.axis_size("dom")))
    node_out, gx, ge, gn = pl.pallas_call(
        functools.partial(layer_kernel, scale),
        out_shape=(
            jax.ShapeDtypeStruct((1024, 256), BF),
            jax.ShapeDtypeStruct((1024, 256), BF),
            jax.ShapeDtypeStruct((16, 16, 256), BF),
            jax.ShapeDtypeStruct((8, 8, 8, 256), BF),
        ),
        in_specs=[hbm, vmem, smem, smem, hbm, hbm, hbm, hbm],
        out_specs=(hbm, hbm, hbm, hbm),
        scratch_shapes=[
            V((1024, 256), BF),
            V((8, 4, 128, 128), BF),
            V((256, 256), BF),
            V((512, 256), BF),
            V((1024, 256), BF),
            V((64, 16, 256), BF),
            V((64, 16, 256), BF),
            V((1024, 256), F32),
            V((1024, 256), BF),
            V((1536, 1024), BF),
            V((8, 128, 512), BF),
            V((1024, 1024), BF),
            V((1024, 256), BF),
            V((1024, 256), F32),
            V((1024, 256), BF),
            V((1024, 256), F32),
            V((2, 256, 256), BF),
            V((2, 256, 256), BF),
            V((12, 128, 256), BF),
            V((1024, 256), BF),
            V((64, 16, 256), BF),
            V((64, 16, 256), BF),
            V((1024, 256), BF),
            V((1024, 256), BF),
            V((2, 4, 8, 8, 256), F32),
            V((16, 16, 256), BF),
            V((4, 8, 8, 256), BF),
            V((4, 8, 8, 256), BF),
            V((4, 8, 8, 256), BF),
            V((4, 8, 8, 256), BF),
            V((16, 16, 256), BF),
            V((8, 8, 256), BF),
            V((8, 16, 256), BF),
            V((8, 8, 256), BF),
            V((8, 8, 256), BF),
            V((8, 8, 256), BF),
            V((4, 16, 256), BF),
            V((8, 8, 8, 256), BF),
            V((16, 16, 256), BF),
            dma((5,)),
            dma(()),
            dma((8,)),
            dma(()),
            dma(()),
            dma((4,)),
            dma((4,)),
            dma((12,)),
            dma((12,)),
            dma((7,)),
        ],
        compiler_params=pltpu.CompilerParams(
            collective_id=0, has_side_effects=True, vmem_limit_bytes=60 << 20
        ),
        name="layer",
    )(
        features[0],
        send_order.reshape(8, 128),
        adj_count,
        adj_target.T,
        adj_vals,
        w_edge,
        w_node,
        cotangent[0],
    )
    return finish(node_out, gx, ge, gn)


def solution(mesh):
    in_specs = (
        P("dp", "dom", None),
        P("dom", None),
        P("dom"),
        P("dom", None),
        P("dom", None, None, None),
        P(),
        P(),
        P("dp", "dom", None),
    )
    out_specs = (P("dp", "dom", None), P("dp", "dom", None), P(), P())
    return jax.shard_map(shards, mesh=mesh, in_specs=in_specs, out_specs=out_specs, check_vma=False)
```
